128 devices in a mesh: surf: 32 (over z_lo, x, y), wall: 4 (over z_hi, core).
Axes of the slice: x: 4, y: 4, z: 4 (z_hi: 2, z_lo: 2; z = z_hi * 2 + z_lo), core: 2. Of those that a mesh axis runs over, the one named last changes fastest.
Arguments:
- flow_state: float32 [5, 128, 256, 512], P(None, 'wall', 'surf'), may hold values from -1 to 6, as said below
- spacing: float32 [128, 256, 512], P('wall', 'surf'), may hold values from 0.6 to 1.8
- bc_kind: int32 [256, 512], P('surf'), may hold values from 0 to 2
- cell_of: int32 [131072], P(('surf', 'wall')), may hold values from 0 to 131071, as said below
- zone_id: int32 [131072], P(('surf', 'wall')), may hold values from 0 to 7
- abl_temp: float32 [64, 131072], P(None, ('surf', 'wall')), may hold values from 0.5 to 2
- conduct: float32 [8], replicated, may hold values from 0.3 to 3
- diffuse: float32 [8], replicated, may hold values from 0.1 to 0.45
- rate: float32 [8], replicated, may hold values from 0.3 to 3
Outputs:
- state_next: float32 [5, 128, 256, 512], P(None, 'wall', 'surf')
- node_shift: float32 [128, 256, 512], P('wall', 'surf')
- ablator_next: float32 [64, 131072], P(None, ('surf', 'wall'))
The draws below stay inside these ranges and needn't reach their ends.
Inputs may be any that keep to these rules, and one draw needn't show every extreme that they name: `cell_of`: each surface cell is named by exactly one column; the columns of one device name exactly 32 cells of every surface tile (tile = cell // 4096). `flow_state`: the density U0 is at least 0.45 and the pressure derived from U is at least 0.37 in every cell.
All inputs are finite; a program needn't handle non-finite values.
Results may differ from the reference program's by a relative error of at most 0.0003.
Values sent between devices are 32-bit elements; how exact they have to be, the bound alone decides.
No kernel may reach another device: no remote copies, remote signals or barrier semaphores. Data moves between devices by JAX's collectives and lax.ppermute only.
A program may use at most 128 MiB of HBM per device.

```python
import math
import jax
import jax.numpy as jnp
from jax import lax

CI = 8
NJ = 512
DEPTH = 64
NZONE = 8
NI = 256
NK = 128
NCOL = 131072
N_SURF = 32
N_WALL = 4


def draw_flow_state(key, part):
    keys = jax.random.split(key, 5)
    shape = (NK, NI, NJ)
    density = jax.random.uniform(keys[0], shape, jnp.float32, 0.7, 1.3)
    velo_x = 0.3 * jax.random.truncated_normal(keys[1], -2.0, 2.0, shape, jnp.float32)
    velo_y = 0.3 * jax.random.truncated_normal(keys[2], -2.0, 2.0, shape, jnp.float32)
    velo_z = 0.3 * jax.random.truncated_normal(keys[3], -2.0, 2.0, shape, jnp.float32)
    pressure = jax.random.uniform(keys[4], shape, jnp.float32, 0.6, 1.4)
    energy = pressure / 0.4 + 0.5 * density * (velo_x * velo_x + velo_y * velo_y + velo_z * velo_z)
    return jnp.stack([density, density * velo_x, density * velo_y, density * velo_z, energy])


def tile_pieces(tile_key, tile_index):
    tile_cells = CI * NJ
    device_count = N_SURF * N_WALL
    shuffled = jax.random.permutation(tile_key, tile_cells).astype(jnp.int32) + tile_index * tile_cells
    return shuffled.reshape(device_count, tile_cells // device_count)


def mix_row(row_key, row_values):
    return jax.random.permutation(row_key, row_values)


def draw_cell_of(key, part):
    device_count = N_SURF * N_WALL
    tile_keys = jax.random.split(jax.random.fold_in(key, 11), N_SURF)
    pieces = jax.vmap(tile_pieces)(tile_keys, jnp.arange(N_SURF, dtype=jnp.int32))
    per_device = jnp.transpose(pieces, (1, 0, 2)).reshape(device_count, -1)
    device_keys = jax.random.split(jax.random.fold_in(key, 23), device_count)
    mixed = jax.vmap(mix_row)(device_keys, per_device)
    return mixed.reshape(-1).astype(jnp.int32)


def set_ends(entries, key, low, high):
    shape = entries.shape
    index_at = [jax.random.randint(jax.random.fold_in(key, axis), (), 0, shape[axis]) for axis in range(len(shape))]
    entries = entries.at[tuple(index_at)].set(low)
    longest = shape.index(max(shape))
    index_at[longest] = (index_at[longest] + 1) % shape[longest]
    return entries.at[tuple(index_at)].set(high)


def level_of(own_key, shape, cuts, least, largest):
    loudness = 1.0
    for axis_at, shards_of in cuts:
        heights = jax.random.uniform(jax.random.fold_in(jax.random.fold_in(own_key, 6), axis_at), (shards_of,), jnp.float32, least / len(cuts), largest / len(cuts))
        loudness = loudness * jnp.repeat(jnp.exp(heights), shape[axis_at] // shards_of).reshape((-1,) + (1,) * (len(shape) - 1 - axis_at))
    return loudness


def setup_inputs(seed: int = 0) -> dict:
    key_of = jax.random.split(jax.random.key(seed), 10)
    return {
        "flow_state": draw_flow_state(jax.random.fold_in(key_of[9], 71), 0),
        "spacing": jnp.clip(0.6 + 1.1999999 * jax.random.uniform(key_of[1], (NK, NI, NJ), jnp.float32) ** level_of(key_of[1], (NK, NI, NJ), ((0, 4), (1, 32)), -0.2, 0.2), 0.6, 1.8),
        "bc_kind": set_ends(jax.random.randint(key_of[2], (NI, NJ), 0, 3), jax.random.fold_in(key_of[2], 1), 0, 2).astype(jnp.int32),
        "cell_of": draw_cell_of(jax.random.fold_in(key_of[9], 71), 0),
        "zone_id": set_ends(jax.random.randint(key_of[4], (NCOL,), 0, NZONE), jax.random.fold_in(key_of[4], 1), 0, NZONE - 1).astype(jnp.int32),
        "abl_temp": jnp.clip(0.5 + 1.5 * jax.random.uniform(key_of[5], (DEPTH, NCOL), jnp.float32) ** level_of(key_of[5], (DEPTH, NCOL), ((1, 128),), -0.2, 0.2), 0.5, 2.0),
        "conduct": jnp.clip(jnp.exp(jax.random.uniform(key_of[6], (NZONE,), jnp.float32, math.log(0.3), math.log(3.0))), 0.3, 3.0),
        "diffuse": jnp.clip(jax.random.uniform(key_of[7], (NZONE,), jnp.float32, 0.1, 0.45), 0.1, 0.45),
        "rate": jnp.clip(jnp.exp(jax.random.uniform(key_of[8], (NZONE,), jnp.float32, math.log(0.3), math.log(3.0))), 0.3, 3.0),
    }


heat_ratio = 1.4
time_step = 0.15
viscosity = 0.05
conduction = 0.07
sponge_rate = 0.5
activation = 2.0
blow_ratio = 1.0
radiation = 0.8
film_conduct = 1.0
recovery = 0.2
far_values = (1.0, 0.5, 0.0, 0.0, 2.625)


def primitives(values):
    density = values[0]
    velo_x = values[1] / density
    velo_y = values[2] / density
    velo_z = values[3] / density
    kinetic = 0.5 * density * (velo_x * velo_x + velo_y * velo_y + velo_z * velo_z)
    pressure = (heat_ratio - 1.0) * (values[4] - kinetic)
    return density, velo_x, velo_y, velo_z, pressure


def conserved(density, velo_x, velo_y, velo_z, pressure):
    energy = pressure / (heat_ratio - 1.0) + 0.5 * density * (velo_x * velo_x + velo_y * velo_y + velo_z * velo_z)
    return jnp.stack([density, density * velo_x, density * velo_y, density * velo_z, energy])


def wall_ghost(cell_row, surf_temp, surf_blow, kind_rows):
    density, velo_x, velo_y, velo_z, pressure = primitives(cell_row)
    wall_density = pressure / surf_temp
    noslip = conserved(wall_density, -velo_x, -velo_y, -velo_z, pressure)
    slip_state = conserved(density, velo_x, velo_y, -velo_z, pressure)
    blow_state = conserved(wall_density, -velo_x, -velo_y, 2.0 * surf_blow - velo_z, pressure)
    return jnp.where(kind_rows == 0, noslip, jnp.where(kind_rows == 1, slip_state, blow_state))


def shifted_slice(padded, along_axis, offset, length):
    return lax.slice_in_dim(padded, 2 + offset, 2 + offset + length, axis=along_axis)


def first_diff(padded, along_axis, length):
    near_diff = shifted_slice(padded, along_axis, 1, length) - shifted_slice(padded, along_axis, -1, length)
    outer_diff = shifted_slice(padded, along_axis, 2, length) - shifted_slice(padded, along_axis, -2, length)
    return (8.0 * near_diff - outer_diff) / 12.0


def second_diff(padded, along_axis, length):
    near_sum = shifted_slice(padded, along_axis, 1, length) + shifted_slice(padded, along_axis, -1, length)
    outer_sum = shifted_slice(padded, along_axis, 2, length) + shifted_slice(padded, along_axis, -2, length)
    return (16.0 * near_sum - outer_sum - 30.0 * shifted_slice(padded, along_axis, 0, length)) / 12.0


def wrap_last(values):
    return jnp.concatenate([values[..., -2:], values, values[..., :2]], axis=-1)


def fluxes(values, normal):
    density, velo_x, velo_y, velo_z, pressure = primitives(values)
    speeds = (velo_x, velo_y, velo_z)
    normal_speed = speeds[normal]
    momentum_flux = [values[1] * normal_speed, values[2] * normal_speed, values[3] * normal_speed]
    momentum_flux[normal] = momentum_flux[normal] + pressure
    face_flux = jnp.stack([values[normal + 1], momentum_flux[0], momentum_flux[1], momentum_flux[2], (values[4] + pressure) * normal_speed])
    lap_fields = jnp.stack([velo_x, velo_y, velo_z, pressure / density])
    return face_flux, lap_fields


def advance(padded_state, padded_heights, normalized):
    depth_k = padded_heights.shape[0] - 4
    rows_i = padded_state.shape[2] - 4
    cols_j = padded_state.shape[3]
    center_state = padded_state[:, 2:-2, 2:-2, :]
    side_state = padded_state[:, 2:-2, :, :]
    stack_state = padded_state[:, :, 2:-2, :]
    flux_i, lap_i = fluxes(side_state, 0)
    flux_j, lap_j = fluxes(wrap_last(center_state), 1)
    flux_k, lap_k = fluxes(stack_state, 2)
    metric = first_diff(padded_heights, 0, depth_k)
    convect = first_diff(flux_i, 2, rows_i) + first_diff(flux_j, 3, cols_j) + first_diff(flux_k, 1, depth_k) / metric
    laplace = second_diff(lap_i, 2, rows_i) + second_diff(lap_j, 3, cols_j) + second_diff(lap_k, 1, depth_k) / (metric * metric)
    viscous = jnp.stack([jnp.zeros_like(laplace[0]), viscosity * laplace[0], viscosity * laplace[1], viscosity * laplace[2], conduction * laplace[3]])
    far_field = jnp.array(far_values, jnp.float32)[:, None, None, None]
    sponge = sponge_rate * normalized * normalized * (center_state - far_field)
    return center_state + time_step * (viscous - convect - sponge)


def ablate(abl_temp, col_film, col_recovery, col_conduct, col_diffuse, col_rate):
    inner_temp = abl_temp[1]
    surface = abl_temp[0]
    for newton_pass in range(2):
        surface_cube = surface * surface * surface
        surface = (col_film * col_recovery + col_conduct * inner_temp + 3.0 * radiation * surface_cube * surface) / (col_film + col_conduct + 4.0 * radiation * surface_cube)
    recession = col_rate * jnp.exp(-activation / surface)
    blowing = blow_ratio * recession
    profile = jnp.concatenate([surface[None], abl_temp[1:]], axis=0)
    for heat_pass in range(2):
        middle = profile[1:-1] + col_diffuse * (profile[2:] - 2.0 * profile[1:-1] + profile[:-2])
        bottom = profile[-1] + 2.0 * col_diffuse * (profile[-2] - profile[-1])
        profile = jnp.concatenate([profile[:1], middle, bottom[None]], axis=0)
    return surface, blowing, recession, profile


def extend_heights(shifted):
    wall_low = jnp.stack([3.0 * shifted[0] - 2.0 * shifted[1], 2.0 * shifted[0] - shifted[1]])
    wall_high = jnp.stack([2.0 * shifted[-1] - shifted[-2], 3.0 * shifted[-1] - 2.0 * shifted[-2]])
    return jnp.concatenate([wall_low, shifted, wall_high], axis=0)


def reference(flow_state, spacing, bc_kind, cell_of, zone_id, abl_temp, conduct, diffuse, rate):
    density, velo_x, velo_y, velo_z, pressure = primitives(flow_state[:, 0])
    recovery_temp = pressure / density + recovery * (velo_x * velo_x + velo_y * velo_y + velo_z * velo_z)
    film = film_conduct / (0.5 * spacing[0])
    col_film = film.reshape(-1)[cell_of]
    col_recovery = recovery_temp.reshape(-1)[cell_of]
    surface, blowing, recession, ablator_next = ablate(abl_temp, col_film, col_recovery, conduct[zone_id], diffuse[zone_id], rate[zone_id])
    cell_count = NI * NJ
    surf_temp = jnp.zeros((cell_count,), jnp.float32).at[cell_of].set(surface).reshape(NI, NJ)
    surf_blow = jnp.zeros((cell_count,), jnp.float32).at[cell_of].set(blowing).reshape(NI, NJ)
    surf_recess = jnp.zeros((cell_count,), jnp.float32).at[cell_of].set(recession).reshape(NI, NJ)
    center = jnp.cumsum(spacing, axis=0) - 0.5 * spacing
    column_total = jnp.sum(spacing, axis=0)
    node_shift = surf_recess * (center / column_total - 1.0)
    shifted = center + node_shift
    normalized = center / column_total

    def one_tile(tile_index):
        first_row = tile_index * CI
        wrapped = (first_row - 2 + jnp.arange(CI + 4, dtype=jnp.int32)) % NI
        tile_block = jnp.take(flow_state, wrapped, axis=2)
        temp_rows = jnp.take(surf_temp, wrapped, axis=0)
        blow_rows = jnp.take(surf_blow, wrapped, axis=0)
        kind_rows = jnp.take(bc_kind, wrapped, axis=0)
        ghost_one = wall_ghost(tile_block[:, 0], temp_rows, blow_rows, kind_rows)
        ghost_two = wall_ghost(tile_block[:, 1], temp_rows, blow_rows, kind_rows)
        far_rows = jnp.broadcast_to(jnp.array(far_values, jnp.float32)[:, None, None, None], (5, 2, CI + 4, NJ))
        padded_state = jnp.concatenate([ghost_two[:, None], ghost_one[:, None], tile_block, far_rows], axis=1)
        heights_block = lax.dynamic_slice_in_dim(shifted, first_row, CI, axis=1)
        norm_block = lax.dynamic_slice_in_dim(normalized, first_row, CI, axis=1)
        return advance(padded_state, extend_heights(heights_block), norm_block)

    blocks = lax.map(one_tile, jnp.arange(N_SURF, dtype=jnp.int32))
    state_next = jnp.moveaxis(blocks, 0, 2).reshape(5, NK, NI, NJ)
    return state_next, node_shift, ablator_next
```

```python
import functools
import jax
import jax.numpy as jnp
from jax import lax
from jax.experimental import pallas as pl
from jax.experimental.pallas import tpu as pltpu
from jax.sharding import PartitionSpec as P

gas = 0.4
time_step = 0.15
viscosity = 0.05
conduction = 0.07
sponge_rate = 0.5
activation = 2.0
radiation = 0.8
recovery = 0.2
far_values = (1.0, 0.5, 0.0, 0.0, 2.625)
diffusivity = (viscosity, viscosity, viscosity, conduction)

F32 = jnp.float32
BF16 = jnp.bfloat16
CHUNK = 4


def iota(shape, axis):
    return lax.broadcasted_iota(jnp.int32, shape, axis)


def split3(x):
    high = x.astype(BF16)
    rest = x - high.astype(F32)
    middle = rest.astype(BF16)
    low = (rest - middle.astype(F32)).astype(BF16)
    return high, middle, low


def dot_nn(a, b):
    return lax.dot_general(a, b, (((1,), (0,)), ((), ())), preferred_element_type=F32)


def dot_nt(a, b):
    return lax.dot_general(a, b, (((1,), (1,)), ((), ())), preferred_element_type=F32)


def join3(x, rows):
    return x[:rows] + x[rows : 2 * rows] + x[2 * rows :]


def to_rows(x):
    return jnp.concatenate([x[:, 128 * c : 128 * c + 128] for c in range(4)], axis=0)


def to_grid(x):
    return jnp.concatenate([x[8 * c : 8 * c + 8] for c in range(4)], axis=1)


def onehot(mask):
    return jnp.where(mask, 1.0, 0.0).astype(BF16)


def primitives(u0, u1, u2, u3, u4):
    inverse = 1.0 / u0
    vx = u1 * inverse
    vy = u2 * inverse
    vz = u3 * inverse
    pressure = gas * (u4 - 0.5 * (u1 * vx + u2 * vy + u3 * vz))
    return inverse, vx, vy, vz, pressure


def pack_kernel(flow, spacing, next_side, prev_side, up_wall, down_wall, wall_fields):
    row = iota((8, 512), 0) // 2
    for m in range(5):

        def gather(block, carry, m=m):
            high = jnp.zeros((8, 512), F32)
            low = jnp.zeros((8, 512), F32)
            for b in range(4):
                plane = flow[m, block * 4 + b]
                rolled_high = pltpu.roll(plane, (2 * b + 2) % 8, 0)
                rolled_low = pltpu.roll(plane, 2 * b, 0) if b else plane
                high = jnp.where(row == b, rolled_high, high)
                low = jnp.where(row == b, rolled_low, low)
            next_side[m, block] = high
            prev_side[m, block] = low
            return carry

        lax.fori_loop(0, 8, gather, 0)
    for m in range(5):
        for layer in range(2):
            up_wall[2 * m + layer] = flow[m, 30 + layer]
            down_wall[2 * m + layer] = flow[m, layer]
    for layer in range(2):
        up_wall[10 + layer] = spacing[30 + layer]
        down_wall[10 + layer] = spacing[layer]
    inverse, vx, vy, vz, pressure = primitives(*[flow[m, 0] for m in range(5)])
    film = 2.0 / spacing[0]
    temp = pressure * inverse + recovery * (vx * vx + vy * vy + vz * vz)
    total = spacing[0]
    for k in range(1, 32):
        total = total + spacing[k]
    for index, value in enumerate((film, temp, total)):
        up_wall[12 + index] = value
        down_wall[12 + index] = value
        wall_fields[index] = value


def route_kernel(cell, zone, temps, outgoing, rank_out):
    cells = cell[...]
    tile = cells // 4096
    within = cells - tile * 4096
    hit = iota((32, 1024), 0) == tile
    ones = jnp.where(hit, 1.0, 0.0)
    stacked = jnp.concatenate([ones[:, 128 * k : 128 * k + 128] for k in range(8)], axis=0)
    inner = iota((128, 256), 0)
    outer = iota((128, 256), 1)
    ahead = onehot((inner < outer) | (outer >= 128))
    counts = dot_nn(stacked.astype(BF16), ahead)
    offset = jnp.zeros((32, 128), F32)
    ranks = []
    for k in range(8):
        part = slice(32 * k, 32 * k + 32)
        place = counts[part, :128] + offset
        ranks.append(jnp.sum(stacked[part] * place, axis=0, keepdims=True))
        offset = offset + counts[part, 128:]
    rank = jnp.concatenate(ranks, axis=1).astype(jnp.int32)
    rank_out[...] = rank
    slot = iota((32, 1024), 0) == rank
    first, second = temps[0:1], temps[1:2]
    fields = (within.astype(F32), (zone[...] + 1).astype(F32), first, second)
    pieces = [split3(value) for value in fields]
    rows = []
    for level in range(3):
        for piece in pieces:
            rows.append(jnp.where(slot, piece[level].astype(F32), 0.0).astype(BF16))
    sent = dot_nt(ones.astype(BF16), jnp.concatenate(rows, axis=0))
    outgoing[...] = sent[:, :128] + sent[:, 128:256] + sent[:, 256:]


def pick_wall(wall, own, low, opposite, high):
    return jnp.where(wall == 0, own, jnp.where(wall == 1, low, jnp.where(wall == 2, opposite, high)))


def surface_kernel(place, conduct, rate, arrived, own, low, opposite, high, dense, where_out):
    wall = place[0]
    received = arrived[...]
    pieces = jnp.concatenate(split3(received), axis=0)
    lane = iota((128, 1024), 1) % 32
    line = iota((128, 1024), 0)
    source = iota((32, 1024), 0) == iota((32, 1024), 1) // 32
    flat = []
    for f in range(4):
        spread = join3(dot_nn(pieces, onehot(line == lane + 32 * f)), 32)
        flat.append(jnp.sum(jnp.where(source, spread, 0.0), axis=0, keepdims=True))
    where_out[...] = flat[0]
    cells = flat[0].astype(jnp.int32)
    block = ((cells % 512) // 128) * 8 + cells // 512
    block_hit = iota((32, 1024), 0) == block
    lane_hit = onehot(line == cells % 128)
    rows = [jnp.where(block_hit, flat[1], 0.0).astype(BF16)]
    for value in flat[2:]:
        for piece in split3(value):
            rows.append(jnp.where(block_hit, piece.astype(F32), 0.0).astype(BF16))
    grid = dot_nt(jnp.concatenate(rows, axis=0), lane_hit)
    zones = to_grid(grid[:32])
    first = to_grid(join3(grid[32:128], 32))
    inner = to_grid(join3(grid[128:], 32))
    film = pick_wall(wall, own[0], low[12], opposite[0], high[12])
    recover = pick_wall(wall, own[1], low[13], opposite[1], high[13])
    cond = jnp.zeros((8, 512), F32)
    speed = jnp.zeros((8, 512), F32)
    for z in range(8):
        cond = jnp.where(zones == z + 1.0, conduct[z], cond)
        speed = jnp.where(zones == z + 1.0, rate[z], speed)
    surface = first
    base = film * recover + cond * inner
    for step in range(2):
        cube = surface * surface * surface
        surface = (base + 3.0 * radiation * cube * surface) / (film + cond + 4.0 * radiation * cube)
    recess = speed * jnp.exp(-activation / surface)
    taken = zones > 0.5
    dense[0] = jnp.where(taken, surface, 0.0)
    dense[1] = jnp.where(taken, recess, 0.0)


def return_kernel(where_in, dense, outgoing):
    cells = where_in[...].astype(jnp.int32)
    block = ((cells % 512) // 128) * 8 + cells // 512
    block_hit = iota((32, 1024), 0) == block
    line = iota((128, 1024), 0)
    lane_hit = onehot(line == cells % 128)
    pieces = jnp.concatenate(split3(to_rows(dense[0])), axis=0)
    spread = join3(dot_nn(pieces, lane_hit), 32)
    flat = jnp.sum(jnp.where(block_hit, spread, 0.0), axis=0, keepdims=True)
    source = iota((32, 1024), 0) == iota((32, 1024), 1) // 32
    rows = [jnp.where(source, piece.astype(F32), 0.0).astype(BF16) for piece in split3(flat)]
    slot = onehot(line == iota((128, 1024), 1) % 32)
    outgoing[...] = join3(dot_nt(jnp.concatenate(rows, axis=0), slot), 32)


def ablate_kernel(diffuse, cell, rank, zone, back, temps, out):
    pieces = jnp.concatenate(split3(back[...]), axis=0)
    slot = onehot(iota((128, 1024), 0) == rank[...])
    spread = join3(dot_nn(pieces, slot), 32)
    tile_hit = iota((32, 1024), 0) == cell[...] // 4096
    surface = jnp.sum(jnp.where(tile_hit, spread, 0.0), axis=0, keepdims=True)
    zones = zone[...]
    spread_rate = jnp.zeros((1, 1024), F32)
    for z in range(8):
        spread_rate = jnp.where(zones == z, diffuse[z], spread_rate)
    row = iota((64, 1024), 0)
    profile = jnp.where(row == 0, surface, temps[...])
    for step in range(2):
        before = pltpu.roll(profile, 1, 0)
        after = pltpu.roll(profile, 63, 0)
        after = jnp.where(row == 63, before, after)
        changed = profile + spread_rate * (after - 2.0 * profile + before)
        profile = jnp.where(row == 0, profile, changed)
    out[...] = profile


def stencil_kernel(
    place, flow, spacing, low, high, opposite, own, base, slope, curve, norm, total_out, fields, gaps, run
):
    wall = place[0]
    step = pl.program_id(0)
    twelfth = time_step / 12.0
    is_low = wall == 0
    is_high = wall == 3
    keep_low = jnp.where(is_low, 0.0, 1.0)

    def store_fields(position, values, keep):
        u0, u1, u2, u3, u4 = values
        inverse, vx, vy, vz, pressure = primitives(*values)
        results = (
            u3,
            u1 * vz,
            u2 * vz,
            u3 * vz + pressure,
            (u4 + pressure) * vz,
            vx,
            vy,
            vz,
            pressure * inverse,
            pressure,
        )
        for index, value in enumerate(results):
            fields[index, position] = value if keep is None else value * keep

    def own_plane(k, carry):
        store_fields(k + 2, [flow[m, k] for m in range(5)], None)
        return carry

    @pl.when(step == 0)
    def first():
        for layer in range(2):
            store_fields(layer, [low[2 * m + layer] for m in range(5)], keep_low)
            top = [jnp.where(is_high, far_values[m], high[2 * m + layer]) for m in range(5)]
            store_fields(34 + layer, top, None)
        lax.fori_loop(0, 2, own_plane, 0)
        before = jnp.where(wall >= 1, low[14], 0.0)
        before = before + jnp.where(wall >= 2, opposite[2], 0.0)
        before = before + jnp.where(wall >= 3, high[14], 0.0)
        run[0] = before
        total = own[2] + low[14] + opposite[2] + high[14]
        run[1] = 1.0 / total
        total_out[...] = total

        def gap(k, carry):
            gaps[k + 2] = 0.5 * (spacing[k] + spacing[k + 1])
            return carry

        lax.fori_loop(0, 31, gap, 0)
        gap_low = gaps[2]
        gap_high = gaps[32]
        gaps[0] = jnp.where(is_low, gap_low, 0.5 * (low[10] + low[11]))
        gaps[1] = jnp.where(is_low, gap_low, 0.5 * (low[11] + spacing[0]))
        gaps[33] = jnp.where(is_high, gap_high, 0.5 * (spacing[31] + high[10]))
        gaps[34] = jnp.where(is_high, gap_high, 0.5 * (high[10] + high[11]))

    ahead = jnp.minimum(step * CHUNK + 2 + CHUNK, 32)
    lax.fori_loop(step * CHUNK + 2, ahead, own_plane, 0)

    row = iota((8, 512), 0)
    inverse_total = run[1]

    def one_plane(b, below):
        k = step * CHUNK + b
        thick = spacing[k]
        center = below + 0.5 * thick
        normal = center * inverse_total
        norm[b] = normal - 1.0
        stretch = 7.0 * (gaps[k + 2] + gaps[k + 1]) - gaps[k + 3] - gaps[k]
        inverse_metric = 12.0 / stretch
        damp = time_step * sponge_rate * normal * normal
        slope_scale = -twelfth * inverse_metric
        curve_scale = twelfth * inverse_metric * inverse_metric
        u = [flow[m, k] for m in range(5)]
        vx, vy, vz, temp, pressure = [fields[m, k + 2] for m in range(5, 10)]
        heat = u[4] + pressure
        shear = u[1] * vy
        flux_i = (u[1], u[1] * vx + pressure, shear, u[1] * vz, heat * vx)
        flux_j = (u[2], shear, u[2] * vy + pressure, u[2] * vz, heat * vy)
        smooth = (None, vx, vy, vz, temp)
        for m in range(5):
            result = u[m] - damp * (u[m] - far_values[m])
            w = smooth[m]
            if w is not None:
                amount = twelfth * diffusivity[m - 1]
                w16 = (16.0 * amount) * w
                w1 = amount * w
                result = result - (60.0 * amount) * w
            for axis, flux in ((0, flux_i[m]), (1, flux_j[m])):
                near = (8.0 * twelfth) * flux
                far = twelfth * flux
                if w is None:
                    sources = (near, -near, -far, far)
                else:
                    sources = (w16 + near, w16 - near, -w1 - far, far - w1)
                if axis == 0:
                    limits = (row != 7, row != 0, row < 6, row >= 2)
                    sources = [jnp.where(limit, value, 0.0) for limit, value in zip(limits, sources)]
                size = (8, 512)[axis]
                for shift, value in zip((1, size - 1, 2, size - 2), sources):
                    result = result + pltpu.roll(value, shift, axis)
            base[m, b] = result
            f = [fields[m, k + o] for o in (0, 1, 3, 4)]
            slope[m, b] = slope_scale * (8.0 * (f[2] - f[1]) - (f[3] - f[0]))
            if w is not None:
                g = [fields[m + 4, k + o] for o in (0, 1, 3, 4)]
                bend = 16.0 * (g[1] + g[2]) - (g[0] + g[3]) - 30.0 * w
                curve[m - 1, b] = (curve_scale * diffusivity[m - 1]) * bend
        return below + thick

    run[0] = lax.fori_loop(0, CHUNK, one_plane, run[0])


def final_kernel(
    place,
    base,
    slope,
    curve,
    norm,
    before,
    after,
    total_ref,
    dense,
    dense_1,
    dense_2,
    dense_3,
    bottom,
    thin,
    kinds,
    out,
    shift_out,
    pull,
):
    wall = place[0]
    step = pl.program_id(0)
    twelfth = time_step / 12.0
    row = iota((8, 512), 0)
    odd = row % 2 == 1
    total = total_ref[...]

    @pl.when(step == 0)
    def first():
        recess = dense[1] + dense_1[1] + dense_2[1] + dense_3[1]
        pull[0] = recess
        pull[1] = total / (total + recess)

    recess = pull[0]
    alpha = pull[1]
    edges = []
    for side, near_sign in ((before, 1.0), (after, -1.0)):
        u = [side[m, 0] for m in range(5)]
        inverse, vx, vy, vz, pressure = primitives(*u)
        flux = (u[1], u[1] * vx + pressure, u[1] * vy, u[1] * vz, (u[4] + pressure) * vx)
        smooth = (None, vx, vy, vz, pressure * inverse)
        results = []
        for m in range(5):
            near = (8.0 * twelfth * near_sign) * flux[m]
            far = (-twelfth * near_sign) * flux[m]
            if smooth[m] is not None:
                amount = twelfth * diffusivity[m - 1]
                near = near + (16.0 * amount) * smooth[m]
                far = far - amount * smooth[m]
            if near_sign > 0:
                moved = jnp.where(odd, 0.0, pltpu.roll(near, 7, 0))
            else:
                moved = jnp.where(odd, pltpu.roll(near, 1, 0), 0.0)
            results.append(far + moved)
        edges.append(results)
    for b in range(CHUNK):
        for m in range(5):
            value = slope[m, b]
            if m:
                value = value + alpha * curve[m - 1, b]
            value = base[m, b] + alpha * value
            low_edge = pltpu.roll(edges[0][m], (8 - 2 * b) % 8, 0) if b else edges[0][m]
            high_edge = pltpu.roll(edges[1][m], (6 - 2 * b) % 8, 0) if b != 3 else edges[1][m]
            value = value + jnp.where(row < 2, low_edge, jnp.where(row >= 6, high_edge, 0.0))
            out[m, b] = value
        shift_out[b] = recess * norm[b]

    @pl.when((step == 0) & (wall == 0))
    def ghosts():
        hot = dense[0] + dense_1[0] + dense_2[0] + dense_3[0]
        kind = kinds[...]
        cooled = 1.0 / hot
        ghost_flux = []
        ghost_smooth = []
        for layer in range(2):
            u = [bottom[m, layer] for m in range(5)]
            inverse, vx, vy, vz, pressure = primitives(*u)
            slip = kind == 1
            density = jnp.where(slip, u[0], pressure * cooled)
            gx = jnp.where(slip, vx, -vx)
            gy = jnp.where(slip, vy, -vy)
            gz = jnp.where(kind == 2, 2.0 * recess - vz, -vz)
            gas_temp = pressure / density
            heat = pressure * (1.0 / gas + 1.0) + 0.5 * density * (gx * gx + gy * gy + gz * gz)
            flow_z = density * gz
            ghost_flux.append((flow_z, flow_z * gx, flow_z * gy, flow_z * gz + pressure, heat * gz))
            ghost_smooth.append((gx, gy, gz, gas_temp))
        gap = [0.5 * (thin[k] + thin[k + 1]) for k in range(3)]
        stretch = (13.0 * gap[0] - gap[1], 7.0 * gap[1] + 6.0 * gap[0] - gap[2])
        for k in range(2):
            scale = alpha * (12.0 / stretch[k])
            for m in range(5):
                near = ghost_flux[0][m]
                if k == 0:
                    value = (-twelfth * scale) * (ghost_flux[1][m] - 8.0 * near)
                else:
                    value = (-twelfth * scale) * near
                if m:
                    close = ghost_smooth[0][m - 1]
                    bend = 16.0 * close - ghost_smooth[1][m - 1] if k == 0 else -close
                    value = value + (twelfth * diffusivity[m - 1]) * scale * scale * bend
                out[m, k] = out[m, k] + value


def whole(shape):
    return pl.BlockSpec(shape, lambda *_: (0,) * len(shape))


SCALARS = pl.BlockSpec(memory_space=pltpu.SMEM)


def params(limit=None):
    return pltpu.CompilerParams(vmem_limit_bytes=limit or 48 * 1024 * 1024)


def cost(flops, moved):
    return pl.CostEstimate(flops=flops, transcendentals=0, bytes_accessed=moved)


def struct(*shape, dtype=F32):
    return jax.ShapeDtypeStruct(shape, dtype)


def shards(flow_state, spacing, bc_kind, cell_of, zone_id, abl_temp, conduct, diffuse, rate):
    surf_count = lax.axis_size("surf")
    wall_count = lax.axis_size("wall")
    place = lax.axis_index("wall").astype(jnp.int32).reshape(1)
    cells = cell_of.reshape(1, 1024)
    zones = zone_id.reshape(1, 1024)

    def turn(value, axis, count, by):
        return lax.ppermute(value, axis, [(i, (i + by) % count) for i in range(count)])

    outgoing, rank = pl.pallas_call(
        route_kernel,
        out_shape=(struct(32, 128), struct(1, 1024, dtype=jnp.int32)),
        in_specs=[
            pl.BlockSpec((1, 1024), lambda i: (0, 0)),
            pl.BlockSpec((1, 1024), lambda i: (0, 0)),
            pl.BlockSpec((8, 1024), lambda i: (0, 0)),
        ],
        out_specs=(whole((32, 128)), whole((1, 1024))),
        grid=(1,),
        compiler_params=params(),
        cost_estimate=cost(4000000, 60000),
        name="route",
    )(cells, zones, abl_temp)
    next_side, prev_side, up_wall, down_wall, wall_fields = pl.pallas_call(
        pack_kernel,
        out_shape=(
            struct(5, 8, 8, 512),
            struct(5, 8, 8, 512),
            struct(15, 8, 512),
            struct(15, 8, 512),
            struct(3, 8, 512),
        ),
        compiler_params=params(),
        cost_estimate=cost(4000000, 5000000),
        name="pack",
    )(flow_state, spacing)
    arrived = lax.all_to_all(outgoing, "surf", split_axis=0, concat_axis=0, tiled=True)
    low = turn(up_wall, "wall", wall_count, 1)
    high = turn(down_wall, "wall", wall_count, wall_count - 1)
    opposite = turn(wall_fields, "wall", wall_count, 2)
    before = turn(next_side, "surf", surf_count, 1)
    after = turn(prev_side, "surf", surf_count, surf_count - 1)

    planes = lambda count: pl.BlockSpec((count, CHUNK, 8, 512), lambda i: (0, i, 0, 0))
    plane = pl.BlockSpec((CHUNK, 8, 512), lambda i: (i, 0, 0))
    base, slope, curve, norm, total = pl.pallas_call(
        stencil_kernel,
        out_shape=(
            struct(5, 32, 8, 512),
            struct(5, 32, 8, 512),
            struct(4, 32, 8, 512),
            struct(32, 8, 512),
            struct(8, 512),
        ),
        grid=(32 // CHUNK,),
        in_specs=[
            SCALARS,
            whole((5, 32, 8, 512)),
            whole((32, 8, 512)),
            whole((15, 8, 512)),
            whole((15, 8, 512)),
            whole((3, 8, 512)),
            whole((3, 8, 512)),
        ],
        out_specs=(planes(5), planes(5), planes(4), plane, whole((8, 512))),
        scratch_shapes=[
            pltpu.VMEM((10, 36, 8, 512), F32),
            pltpu.VMEM((35, 8, 512), F32),
            pltpu.VMEM((2, 8, 512), F32),
        ],
        compiler_params=params(),
        cost_estimate=cost(50000000, 11000000),
        name="stencil",
    )(place, flow_state, spacing, low, high, opposite, wall_fields)

    dense, where_cells = pl.pallas_call(
        surface_kernel,
        out_shape=(struct(2, 8, 512), struct(1, 1024)),
        in_specs=[SCALARS, SCALARS, SCALARS] + [pl.BlockSpec(memory_space=pltpu.VMEM)] * 5,
        compiler_params=params(),
        cost_estimate=cost(4000000, 600000),
        name="surface",
    )(place, conduct, rate, arrived, wall_fields, low, opposite, high)
    dense_1 = turn(dense, "wall", wall_count, 1)
    dense_2 = turn(dense, "wall", wall_count, 2)
    dense_3 = turn(dense, "wall", wall_count, 3)
    returned = pl.pallas_call(
        return_kernel,
        out_shape=struct(32, 128),
        compiler_params=params(),
        cost_estimate=cost(4000000, 60000),
        name="answer",
    )(where_cells, dense)
    back = lax.all_to_all(returned, "surf", split_axis=0, concat_axis=0, tiled=True)

    state_next, node_shift = pl.pallas_call(
        final_kernel,
        out_shape=(struct(5, 32, 8, 512), struct(32, 8, 512)),
        grid=(32 // CHUNK,),
        in_specs=[
            SCALARS,
            planes(5),
            planes(5),
            planes(4),
            plane,
            pl.BlockSpec((5, 1, 8, 512), lambda i: (0, i, 0, 0)),
            pl.BlockSpec((5, 1, 8, 512), lambda i: (0, i, 0, 0)),
            whole((8, 512)),
            whole((2, 8, 512)),
            whole((2, 8, 512)),
            whole((2, 8, 512)),
            whole((2, 8, 512)),
            whole((5, 4, 8, 512)),
            whole((4, 8, 512)),
            whole((8, 512)),
        ],
        out_specs=(planes(5), plane),
        scratch_shapes=[pltpu.VMEM((2, 8, 512), F32)],
        compiler_params=params(),
        cost_estimate=cost(20000000, 14000000),
        name="final",
    )(
        place,
        base,
        slope,
        curve,
        norm,
        before,
        after,
        total,
        dense,
        dense_1,
        dense_2,
        dense_3,
        flow_state,
        spacing,
        bc_kind,
    )
    ablator_next = pl.pallas_call(
        ablate_kernel,
        out_shape=struct(64, 1024),
        in_specs=[SCALARS] + [pl.BlockSpec(memory_space=pltpu.VMEM)] * 5,
        compiler_params=params(),
        cost_estimate=cost(4000000, 600000),
        name="ablate",
    )(diffuse, cells, rank, zones, back, abl_temp)
    return (state_next, node_shift, ablator_next)


def solution(mesh):
    in_specs = (
        P(None, "wall", "surf", None),
        P("wall", "surf", None),
        P("surf", None),
        P(("surf", "wall")),
        P(("surf", "wall")),
        P(None, ("surf", "wall")),
        P(),
        P(),
        P(),
    )
    out_specs = (P(None, "wall", "surf", None), P("wall", "surf", None), P(None, ("surf", "wall")))
    return jax.shard_map(shards, mesh=mesh, in_specs=in_specs, out_specs=out_specs, check_vma=False)
```

```python
import functools
import jax
import jax.numpy as jnp
from jax import lax
from jax.experimental import pallas as pl
from jax.experimental.pallas import tpu as pltpu
from jax.sharding import PartitionSpec as P

gas = 0.4
time_step = 0.15
viscosity = 0.05
conduction = 0.07
sponge_rate = 0.5
activation = 2.0
radiation = 0.8
recovery = 0.2
far_values = (1.0, 0.5, 0.0, 0.0, 2.625)
diffusivity = (viscosity, viscosity, viscosity, conduction)

F32 = jnp.float32
BF16 = jnp.bfloat16


def iota(shape, axis):
    return lax.broadcasted_iota(jnp.int32, shape, axis)


def split3(x):
    high = x.astype(BF16)
    rest = x - high.astype(F32)
    middle = rest.astype(BF16)
    low = (rest - middle.astype(F32)).astype(BF16)
    return high, middle, low


def dot_nn(a, b):
    return lax.dot_general(a, b, (((1,), (0,)), ((), ())), preferred_element_type=F32)


def dot_nt(a, b):
    return lax.dot_general(a, b, (((1,), (1,)), ((), ())), preferred_element_type=F32)


def join3(x, rows):
    return x[:rows] + x[rows : 2 * rows] + x[2 * rows :]


def to_rows(x):
    return jnp.concatenate([x[:, 128 * c : 128 * c + 128] for c in range(4)], axis=0)


def to_grid(x):
    return jnp.concatenate([x[8 * c : 8 * c + 8] for c in range(4)], axis=1)


def onehot(mask):
    return jnp.where(mask, 1.0, 0.0).astype(BF16)


def primitives(u0, u1, u2, u3, u4):
    inverse = 1.0 / u0
    vx = u1 * inverse
    vy = u2 * inverse
    vz = u3 * inverse
    pressure = gas * (u4 - 0.5 * (u1 * vx + u2 * vy + u3 * vz))
    return inverse, vx, vy, vz, pressure


def start_all(copies):
    for copy in copies:
        copy.start()


def wait_all(copies):
    for copy in copies:
        copy.wait()


def pack_kernel(token, flow_hbm, next_hbm, prev_hbm, flow, next_side, prev_side, in_sem, out_sem):
    loads = [
        pltpu.make_async_copy(flow_hbm.at[:, pl.ds(8 * c, 8)], flow.at[:, pl.ds(8 * c, 8)], in_sem.at[c])
        for c in range(4)
    ]
    start_all(loads)
    row = iota((8, 512), 0) // 2
    stores = []
    for c in range(4):
        loads[c].wait()

        def field(m, carry, c=c):
            for block in (2 * c, 2 * c + 1):
                high = jnp.zeros((8, 512), F32)
                low = jnp.zeros((8, 512), F32)
                for b in range(4):
                    plane = flow[m, block * 4 + b]
                    rolled_high = pltpu.roll(plane, (2 * b + 2) % 8, 0) if b != 3 else plane
                    rolled_low = pltpu.roll(plane, 2 * b, 0) if b else plane
                    high = jnp.where(row == b, rolled_high, high)
                    low = jnp.where(row == b, rolled_low, low)
                next_side[m, block] = high
                prev_side[m, block] = low
            return carry

        lax.fori_loop(0, 5, field, 0)
        part = pl.ds(2 * c, 2)
        for side, (here, there) in enumerate(((next_side, next_hbm), (prev_side, prev_hbm))):
            copy = pltpu.make_async_copy(here.at[:, part], there.at[:, part], out_sem.at[side, c])
            copy.start()
            stores.append(copy)
    wait_all(stores)


def route_kernel(cell, zone, temps, outgoing, rank_out):
    cells = cell[...]
    tile = cells // 4096
    within = cells - tile * 4096
    hit = iota((32, 1024), 0) == tile
    ones = jnp.where(hit, 1.0, 0.0)
    stacked = jnp.concatenate([ones[:, 128 * k : 128 * k + 128] for k in range(8)], axis=0)
    inner = iota((128, 256), 0)
    outer = iota((128, 256), 1)
    ahead = onehot((inner < outer) | (outer >= 128))
    counts = dot_nn(stacked.astype(BF16), ahead)
    offset = jnp.zeros((32, 128), F32)
    ranks = []
    for k in range(8):
        part = slice(32 * k, 32 * k + 32)
        place = counts[part, :128] + offset
        ranks.append(jnp.sum(stacked[part] * place, axis=0, keepdims=True))
        offset = offset + counts[part, 128:]
    rank = jnp.concatenate(ranks, axis=1).astype(jnp.int32)
    rank_out[...] = rank
    slot = iota((32, 1024), 0) == rank
    first, second = temps[0:1], temps[1:2]
    fields = (within.astype(F32), (zone[...] + 1).astype(F32), first, second)
    pieces = [split3(value) for value in fields]
    rows = []
    for level in range(3):
        for piece in pieces:
            rows.append(jnp.where(slot, piece[level].astype(F32), 0.0).astype(BF16))
    sent = dot_nt(ones.astype(BF16), jnp.concatenate(rows, axis=0))
    outgoing[...] = sent[:, :128] + sent[:, 128:256] + sent[:, 256:]


def scatter_kernel(
    token, arrived, flow_low, flow_high, spacing, up_wall, down_wall, wall_fields, where_out
):
    for m in range(5):
        for layer in range(2):
            up_wall[2 * m + layer] = flow_high[m, layer]
            down_wall[2 * m + layer] = flow_low[m, layer]
    for layer in range(2):
        up_wall[10 + layer] = spacing[30 + layer]
        down_wall[10 + layer] = spacing[layer]
    inverse, vx, vy, vz, pressure = primitives(*[flow_low[m, 0] for m in range(5)])
    film = 2.0 / spacing[0]
    temp = pressure * inverse + recovery * (vx * vx + vy * vy + vz * vz)
    total = spacing[0]
    for k in range(1, 32):
        total = total + spacing[k]
    received = arrived[...]
    pieces = jnp.concatenate(split3(received), axis=0)
    lane = iota((128, 1024), 1) % 32
    line = iota((128, 1024), 0)
    source = iota((32, 1024), 0) == iota((32, 1024), 1) // 32
    flat = []
    for f in range(4):
        spread = join3(dot_nn(pieces, onehot(line == lane + 32 * f)), 32)
        flat.append(jnp.sum(jnp.where(source, spread, 0.0), axis=0, keepdims=True))
    where_out[...] = flat[0]
    cells = flat[0].astype(jnp.int32)
    block = ((cells % 512) // 128) * 8 + cells // 512
    block_hit = iota((32, 1024), 0) == block
    lane_hit = onehot(line == cells % 128)
    rows = [jnp.where(block_hit, flat[1], 0.0).astype(BF16)]
    for value in flat[2:]:
        for piece in split3(value):
            rows.append(jnp.where(block_hit, piece.astype(F32), 0.0).astype(BF16))
    grid = dot_nt(jnp.concatenate(rows, axis=0), lane_hit)
    zones = to_grid(grid[:32])
    first = to_grid(join3(grid[32:128], 32))
    inner = to_grid(join3(grid[128:], 32))
    for index, value in enumerate((film, temp, total, zones, first, inner)):
        up_wall[12 + index] = value
        down_wall[12 + index] = value
        wall_fields[index] = value


def surface_kernel(
    place, conduct, rate, token, where_in, own, low, opposite, high, surface_out, outgoing
):
    wall = place[0]

    def from_bottom(f):
        return jnp.where(
            wall == 0,
            own[f],
            jnp.where(wall == 1, low[12 + f], jnp.where(wall == 2, opposite[f], high[12 + f])),
        )

    def everywhere(f):
        return (own[f] + low[12 + f]) + (opposite[f] + high[12 + f])

    film = from_bottom(0)
    recover = from_bottom(1)
    below = jnp.where(wall >= 1, low[14], 0.0)
    below = below + jnp.where(wall >= 2, opposite[2], 0.0)
    below = below + jnp.where(wall >= 3, high[14], 0.0)
    zones = everywhere(3)
    surface = everywhere(4)
    inner = everywhere(5)
    cond = jnp.zeros((8, 512), F32)
    speed = jnp.zeros((8, 512), F32)
    for z in range(8):
        cond = jnp.where(zones == z + 1.0, conduct[z], cond)
        speed = jnp.where(zones == z + 1.0, rate[z], speed)
    base = film * recover + cond * inner
    for step in range(2):
        cube = surface * surface * surface
        surface = (base + 3.0 * radiation * cube * surface) / (film + cond + 4.0 * radiation * cube)
    surface_out[0] = surface
    surface_out[1] = speed * jnp.exp(-activation / surface)
    surface_out[2] = everywhere(2)
    surface_out[3] = below
    cells = where_in[...].astype(jnp.int32)
    block = ((cells % 512) // 128) * 8 + cells // 512
    block_hit = iota((32, 1024), 0) == block
    line = iota((128, 1024), 0)
    lane_hit = onehot(line == cells % 128)
    pieces = jnp.concatenate(split3(to_rows(surface)), axis=0)
    spread = join3(dot_nn(pieces, lane_hit), 32)
    flat = jnp.sum(jnp.where(block_hit, spread, 0.0), axis=0, keepdims=True)
    source = iota((32, 1024), 0) == iota((32, 1024), 1) // 32
    rows = [jnp.where(source, piece.astype(F32), 0.0).astype(BF16) for piece in split3(flat)]
    slot = onehot(line == iota((128, 1024), 1) % 32)
    outgoing[...] = join3(dot_nt(jnp.concatenate(rows, axis=0), slot), 32)


def ablate_kernel(diffuse, token, cell, rank, zone, back, temps, out):
    pieces = jnp.concatenate(split3(back[...]), axis=0)
    slot = onehot(iota((128, 1024), 0) == rank[...])
    spread = join3(dot_nn(pieces, slot), 32)
    tile_hit = iota((32, 1024), 0) == cell[...] // 4096
    surface = jnp.sum(jnp.where(tile_hit, spread, 0.0), axis=0, keepdims=True)
    zones = zone[...]
    spread_rate = jnp.zeros((1, 1024), F32)
    for z in range(8):
        spread_rate = jnp.where(zones == z, diffuse[z], spread_rate)
    row = iota((64, 1024), 0)
    profile = jnp.where(row == 0, surface, temps[...])
    for step in range(2):
        before = pltpu.roll(profile, 1, 0)
        after = pltpu.roll(profile, 63, 0)
        after = jnp.where(row == 63, before, after)
        changed = profile + spread_rate * (after - 2.0 * profile + before)
        profile = jnp.where(row == 0, profile, changed)
    out[...] = profile


def chunk_of(ref, c):
    return ref.at[:, pl.ds(8 * c, 8)]


TWELFTH = time_step / 12.0


def side_kernel(flow_hbm, base_hbm, flow, base, in_sem, out_sem):
    loads = [
        pltpu.make_async_copy(chunk_of(flow_hbm, c), chunk_of(flow, c), in_sem.at[c]) for c in range(4)
    ]
    start_all(loads)
    row = iota((8, 512), 0)
    limits = (row != 7, row != 0, row < 6, row >= 2)

    def one_plane(k, carry):
        u = [flow[m, k] for m in range(5)]
        inverse, vx, vy, vz, pressure = primitives(*u)
        temp = pressure * inverse
        heat = u[4] + pressure
        shear = u[1] * vy
        flux_i = (u[1], u[1] * vx + pressure, shear, u[1] * vz, heat * vx)
        flux_j = (u[2], shear, u[2] * vy + pressure, u[2] * vz, heat * vy)
        smooth = (None, vx, vy, vz, temp)
        for m in range(5):
            result = u[m]
            w = smooth[m]
            if w is not None:
                amount = TWELFTH * diffusivity[m - 1]
                w16 = (16.0 * amount) * w
                w1 = amount * w
                result = result - (60.0 * amount) * w
            for axis, flux in ((0, flux_i[m]), (1, flux_j[m])):
                near = (8.0 * TWELFTH) * flux
                far = TWELFTH * flux
                if w is None:
                    sources = (near, -near, -far, far)
                else:
                    sources = (w16 + near, w16 - near, -w1 - far, far - w1)
                if axis == 0:
                    sources = [jnp.where(limit, value, 0.0) for limit, value in zip(limits, sources)]
                size = (8, 512)[axis]
                for shift, value in zip((1, size - 1, 2, size - 2), sources):
                    result = result + pltpu.roll(value, shift, axis)
            base[m, k] = result
        return carry

    stores = []
    for c in range(4):
        loads[c].wait()
        lax.fori_loop(8 * c, 8 * c + 8, one_plane, 0)
        copy = pltpu.make_async_copy(chunk_of(base, c), chunk_of(base_hbm, c), out_sem.at[c])
        copy.start()
        stores.append(copy)
    wait_all(stores)


def normal_flux(u3, density_x, density_y, vx, vy, vz, pressure, heat):
    return (u3, density_x * vz, density_y * vz, u3 * vz + pressure, heat * vz)


def normal_kernel(
    token, flow_hbm, slope_hbm, curve_hbm, flow, fields, slope, curve, in_sem, out_sem
):
    loads = [
        pltpu.make_async_copy(chunk_of(flow_hbm, c), chunk_of(flow, c), in_sem.at[c]) for c in range(4)
    ]
    start_all(loads)
    for f in range(9):
        for edge in (0, 1, 34, 35):
            fields[f, edge] = jnp.zeros((8, 512), F32)

    def one_field(k, carry):
        u = [flow[m, k] for m in range(5)]
        inverse, vx, vy, vz, pressure = primitives(*u)
        values = normal_flux(u[3], u[1], u[2], vx, vy, vz, pressure, u[4] + pressure)
        for index, value in enumerate(values + (vx, vy, vz, pressure * inverse)):
            fields[index, k + 2] = value
        return carry

    def one_plane(k, carry):
        for m in range(5):
            f = [fields[m, k + o] for o in (0, 1, 3, 4)]
            slope[m, k] = 8.0 * (f[2] - f[1]) - (f[3] - f[0])
        for m in range(4):
            g = [fields[m + 5, k + o] for o in range(5)]
            curve[m, k] = 16.0 * (g[1] + g[3]) - (g[0] + g[4]) - 30.0 * g[2]
        return carry

    stores = []
    for c in range(4):
        loads[c].wait()
        lax.fori_loop(8 * c, 8 * c + 8, one_field, 0)
        first = 8 * c - 2 if c else 0
        last = 8 * c + 6 if c < 3 else 32
        lax.fori_loop(first, last, one_plane, 0)
        if c:
            for index, (here, there) in enumerate(((slope, slope_hbm), (curve, curve_hbm))):
                copy = pltpu.make_async_copy(
                    chunk_of(here, c - 1), chunk_of(there, c - 1), out_sem.at[index, c - 1]
                )
                copy.start()
                stores.append(copy)
    for index, (here, there) in enumerate(((slope, slope_hbm), (curve, curve_hbm))):
        copy = pltpu.make_async_copy(chunk_of(here, 3), chunk_of(there, 3), out_sem.at[index, 3])
        copy.start()
        stores.append(copy)
    wait_all(stores)


def final_kernel(
    place,
    surface_hbm,
    low_hbm,
    high_hbm,
    kinds_hbm,
    spacing_hbm,
    flow_hbm,
    base_hbm,
    slope_hbm,
    curve_hbm,
    before_hbm,
    after_hbm,
    out_hbm,
    shift_hbm,
    surface,
    low,
    high,
    kinds,
    thick,
    flow,
    base,
    slope,
    curve,
    before,
    after,
    edges,
    run,
    shift,
    small_sem,
    in_sem,
    side_sem,
    out_sem,
    shift_sem,
):
    wall = place[0]
    small = [
        pltpu.make_async_copy(source, target, small_sem.at[index])
        for index, (source, target) in enumerate(
            (
                (surface_hbm, surface),
                (low_hbm.at[pl.ds(0, 12)], low),
                (high_hbm.at[pl.ds(0, 12)], high),
                (kinds_hbm, kinds),
                (spacing_hbm, thick.at[pl.ds(2, 32)]),
            )
        )
    ]
    start_all(small)
    loads = []
    for c in range(4):
        part = [
            pltpu.make_async_copy(chunk_of(source, c), chunk_of(target, c), in_sem.at[index, c])
            for index, (source, target) in enumerate(
                ((flow_hbm, flow), (slope_hbm, slope), (curve_hbm, curve), (base_hbm, base))
            )
        ]
        for index, (source, target) in enumerate(((before_hbm, before), (after_hbm, after))):
            part.append(
                pltpu.make_async_copy(
                    source.at[:, pl.ds(2 * c, 2)], target.at[:, pl.ds(2 * c, 2)], side_sem.at[index, c]
                )
            )
        start_all(part)
        loads.append(part)
    row = iota((8, 512), 0)
    odd = row % 2 == 1
    wait_all(small)
    is_low = wall == 0
    is_high = wall == 3
    hot = surface[0]
    recess = surface[1]
    total = surface[2]
    alpha = total / (total + recess)
    inverse_total = 1.0 / total
    run[0] = surface[3]
    run[1] = alpha
    run[2] = inverse_total
    thick[0] = jnp.where(is_low, thick[2], low[10])
    thick[1] = jnp.where(is_low, thick[3], low[11])
    thick[34] = jnp.where(is_high, thick[32], high[10])
    thick[35] = jnp.where(is_high, thick[33], high[11])

    def add_edges(near, far, direction, planes):
        near_flux, near_smooth = near
        far_flux, far_smooth = far
        for m in range(5):
            slope[m, planes[0]] += direction * (8.0 * near_flux[m] - far_flux[m])
            slope[m, planes[1]] += direction * (-near_flux[m])
        for m in range(4):
            curve[m, planes[0]] += 16.0 * near_smooth[m] - far_smooth[m]
            curve[m, planes[1]] += -near_smooth[m]

    def low_side():
        kind = kinds[...]
        cooled = 1.0 / hot
        slip = is_low & (kind == 1)
        blow = is_low & (kind == 2)
        sign = jnp.where(is_low, -1.0, 1.0)
        sides = []
        for layer in range(2):
            u = [jnp.where(is_low, flow[m, layer], low[2 * m + 1 - layer]) for m in range(5)]
            inverse, vx, vy, vz, pressure = primitives(*u)
            density = jnp.where(slip | jnp.logical_not(is_low), u[0], pressure * cooled)
            gx = jnp.where(slip, vx, sign * vx)
            gy = jnp.where(slip, vy, sign * vy)
            gz = jnp.where(blow, 2.0 * recess, 0.0) + sign * vz
            heat = pressure * (1.0 / gas + 1.0) + 0.5 * density * (gx * gx + gy * gy + gz * gz)
            flux = normal_flux(density * gz, density * gx, density * gy, gx, gy, gz, pressure, heat)
            sides.append((flux, (gx, gy, gz, pressure / density)))
        add_edges(sides[0], sides[1], -1.0, (0, 1))

    def high_side():
        sides = []
        for layer in range(2):
            u = [jnp.where(is_high, far_values[m], high[2 * m + layer]) for m in range(5)]
            inverse, vx, vy, vz, pressure = primitives(*u)
            flux = normal_flux(u[3], u[1], u[2], vx, vy, vz, pressure, u[4] + pressure)
            sides.append((flux, (vx, vy, vz, pressure * inverse)))
        add_edges(sides[0], sides[1], 1.0, (31, 30))

    def one_block(block, carry):
        for side, (source, near_sign) in enumerate(((before, 1.0), (after, -1.0))):
            u = [source[m, block] for m in range(5)]
            inverse, vx, vy, vz, pressure = primitives(*u)
            flux = (u[1], u[1] * vx + pressure, u[1] * vy, u[1] * vz, (u[4] + pressure) * vx)
            smooth = (None, vx, vy, vz, pressure * inverse)
            for m in range(5):
                near = (8.0 * TWELFTH * near_sign) * flux[m]
                far = (-TWELFTH * near_sign) * flux[m]
                if smooth[m] is not None:
                    amount = TWELFTH * diffusivity[m - 1]
                    near = near + (16.0 * amount) * smooth[m]
                    far = far - amount * smooth[m]
                if near_sign > 0:
                    moved = jnp.where(odd, 0.0, pltpu.roll(near, 7, 0))
                else:
                    moved = jnp.where(odd, pltpu.roll(near, 1, 0), 0.0)
                edges[side, m] = far + moved
        for b in range(4):
            k = block * 4 + b
            width = thick[k + 2]
            center = run[0] + 0.5 * width
            run[0] = run[0] + width
            normal = center * run[2]
            shift[k] = surface[1] * (normal - 1.0)
            stretch = 7.0 * width + 3.0 * (thick[k + 1] + thick[k + 3]) - 0.5 * (thick[k] + thick[k + 4])
            factor = run[1] * (12.0 / stretch)
            damp = (time_step * sponge_rate) * (normal * normal)
            slope_scale = -TWELFTH * factor
            curve_scale = TWELFTH * (factor * factor)
            for m in range(5):
                value = base[m, k] + slope_scale * slope[m, k] - damp * (flow[m, k] - far_values[m])
                if m:
                    value = value + (curve_scale * diffusivity[m - 1]) * curve[m - 1, k]
                low_edge = pltpu.roll(edges[0, m], 8 - 2 * b, 0) if b else edges[0, m]
                high_edge = pltpu.roll(edges[1, m], (6 - 2 * b) % 8, 0) if b != 3 else edges[1, m]
                base[m, k] = value + jnp.where(row < 2, low_edge, jnp.where(row >= 6, high_edge, 0.0))
        return carry

    stores = []
    for c in range(4):
        wait_all(loads[c])
        if c == 0:
            low_side()
        if c == 3:
            high_side()
        lax.fori_loop(2 * c, 2 * c + 2, one_block, 0)
        for copy in (
            pltpu.make_async_copy(chunk_of(base, c), chunk_of(out_hbm, c), out_sem.at[c]),
            pltpu.make_async_copy(
                shift.at[pl.ds(8 * c, 8)], shift_hbm.at[pl.ds(8 * c, 8)], shift_sem.at[c]
            ),
        ):
            copy.start()
            stores.append(copy)
    wait_all(stores)


def whole(shape):
    return pl.BlockSpec(shape, lambda *_: (0,) * len(shape))


SCALARS = pl.BlockSpec(memory_space=pltpu.SMEM)
ANY = pl.BlockSpec(memory_space=pl.ANY)
VMEM = pl.BlockSpec(memory_space=pltpu.VMEM)


def params():
    return pltpu.CompilerParams(vmem_limit_bytes=63 * 1024 * 1024)


def cost():
    return pl.CostEstimate(flops=1000, transcendentals=0, bytes_accessed=1000)


def struct(*shape, dtype=F32):
    return jax.ShapeDtypeStruct(shape, dtype)


def call(kernel, name, out_shape, **options):
    return pl.pallas_call(
        kernel, out_shape=out_shape, name=name, compiler_params=params(), cost_estimate=cost(), **options
    )


def scratch(*shape):
    return pltpu.VMEM(shape, F32)


def copies(*shape):
    return pltpu.SemaphoreType.DMA(shape)


def shards(flow_state, spacing, bc_kind, cell_of, zone_id, abl_temp, conduct, diffuse, rate):
    surf_count = lax.axis_size("surf")
    wall_count = lax.axis_size("wall")
    place = lax.axis_index("wall").astype(jnp.int32).reshape(1)
    cells = cell_of.reshape(1, 1024)
    zones = zone_id.reshape(1, 1024)

    def turn(value, axis, count, by):
        return lax.ppermute(value, axis, [(i, (i + by) % count) for i in range(count)])

    outgoing, rank = call(
        route_kernel,
        "route",
        (struct(32, 128), struct(1, 1024, dtype=jnp.int32)),
        in_specs=[
            pl.BlockSpec((1, 1024), lambda i: (0, 0)),
            pl.BlockSpec((1, 1024), lambda i: (0, 0)),
            pl.BlockSpec((8, 1024), lambda i: (0, 0)),
        ],
        out_specs=(whole((32, 128)), whole((1, 1024))),
        grid=(1,),
    )(cells, zones, abl_temp)
    arrived = lax.all_to_all(outgoing, "surf", split_axis=0, concat_axis=0, tiled=True)
    next_side, prev_side = call(
        pack_kernel,
        "pack",
        (struct(5, 8, 8, 512), struct(5, 8, 8, 512)),
        in_specs=[ANY, ANY],
        out_specs=(ANY, ANY),
        scratch_shapes=[
            scratch(5, 32, 8, 512),
            scratch(5, 8, 8, 512),
            scratch(5, 8, 8, 512),
            copies(4),
            copies(2, 4),
        ],
    )(rank, flow_state)
    before = turn(next_side, "surf", surf_count, 1)
    after = turn(prev_side, "surf", surf_count, surf_count - 1)
    base = call(
        side_kernel,
        "side",
        struct(5, 32, 8, 512),
        in_specs=[ANY],
        out_specs=ANY,
        scratch_shapes=[scratch(5, 32, 8, 512), scratch(5, 32, 8, 512), copies(4), copies(4)],
    )(flow_state)
    up_wall, down_wall, wall_fields, where_cells = call(
        scatter_kernel,
        "scatter",
        (struct(18, 8, 512), struct(18, 8, 512), struct(6, 8, 512), struct(1, 1024)),
        in_specs=[
            ANY,
            whole((32, 128)),
            pl.BlockSpec((5, 2, 8, 512), lambda i: (0, 0, 0, 0)),
            pl.BlockSpec((5, 2, 8, 512), lambda i: (0, 15, 0, 0)),
            whole((32, 8, 512)),
        ],
        out_specs=(whole((18, 8, 512)), whole((18, 8, 512)), whole((6, 8, 512)), whole((1, 1024))),
        grid=(1,),
    )(base, arrived, flow_state, flow_state, spacing)
    low = turn(up_wall, "wall", wall_count, 1)
    high = turn(down_wall, "wall", wall_count, wall_count - 1)
    opposite = turn(wall_fields, "wall", wall_count, 2)
    slope, curve = call(
        normal_kernel,
        "normal",
        (struct(5, 32, 8, 512), struct(4, 32, 8, 512)),
        in_specs=[ANY, ANY],
        out_specs=(ANY, ANY),
        scratch_shapes=[
            scratch(5, 32, 8, 512),
            scratch(9, 36, 8, 512),
            scratch(5, 32, 8, 512),
            scratch(4, 32, 8, 512),
            copies(4),
            copies(2, 4),
        ],
    )(where_cells, flow_state)
    surface, returned = call(
        surface_kernel,
        "surface",
        (struct(4, 8, 512), struct(32, 128)),
        in_specs=[SCALARS] * 3 + [ANY] + [VMEM] * 5,
    )(place, conduct, rate, slope, where_cells, wall_fields, low, opposite, high)
    back = lax.all_to_all(returned, "surf", split_axis=0, concat_axis=0, tiled=True)
    state_next, node_shift = call(
        final_kernel,
        "final",
        (struct(5, 32, 8, 512), struct(32, 8, 512)),
        in_specs=[SCALARS] + [ANY] * 11,
        out_specs=(ANY, ANY),
        scratch_shapes=[
            scratch(4, 8, 512),
            scratch(12, 8, 512),
            scratch(12, 8, 512),
            pltpu.VMEM((8, 512), jnp.int32),
            scratch(36, 8, 512),
            scratch(5, 32, 8, 512),
            scratch(5, 32, 8, 512),
            scratch(5, 32, 8, 512),
            scratch(4, 32, 8, 512),
            scratch(5, 8, 8, 512),
            scratch(5, 8, 8, 512),
            scratch(2, 5, 8, 512),
            scratch(3, 8, 512),
            scratch(32, 8, 512),
            copies(5),
            copies(4, 4),
            copies(2, 4),
            copies(4),
            copies(4),
        ],
    )(place, surface, low, high, bc_kind, spacing, flow_state, base, slope, curve, before, after)
    ablator_next = call(
        ablate_kernel,
        "ablate",
        struct(64, 1024),
        in_specs=[SCALARS, ANY] + [VMEM] * 5,
    )(diffuse, node_shift, cells, rank, zones, back, abl_temp)
    return (state_next, node_shift, ablator_next)


def solution(mesh):
    in_specs = (
        P(None, "wall", "surf", None),
        P("wall", "surf", None),
        P("surf", None),
        P(("surf", "wall")),
        P(("surf", "wall")),
        P(None, ("surf", "wall")),
        P(),
        P(),
        P(),
    )
    out_specs = (P(None, "wall", "surf", None), P("wall", "surf", None), P(None, ("surf", "wall")))
    return jax.shard_map(shards, mesh=mesh, in_specs=in_specs, out_specs=out_specs, check_vma=False)
```

```python
import functools
import jax
import jax.numpy as jnp
from jax import lax
from jax.experimental import pallas as pl
from jax.experimental.pallas import tpu as pltpu
from jax.sharding import PartitionSpec as P

gas = 0.4
time_step = 0.15
viscosity = 0.05
conduction = 0.07
sponge_rate = 0.5
activation = 2.0
radiation = 0.8
recovery = 0.2
far_values = (1.0, 0.5, 0.0, 0.0, 2.625)
diffusivity = (viscosity, viscosity, viscosity, conduction)

F32 = jnp.float32
BF16 = jnp.bfloat16


def iota(shape, axis):
    return lax.broadcasted_iota(jnp.int32, shape, axis)


def split3(x):
    high = x.astype(BF16)
    rest = x - high.astype(F32)
    middle = rest.astype(BF16)
    low = (rest - middle.astype(F32)).astype(BF16)
    return high, middle, low


def dot_nn(a, b):
    return lax.dot_general(a, b, (((1,), (0,)), ((), ())), preferred_element_type=F32)


def dot_nt(a, b):
    return lax.dot_general(a, b, (((1,), (1,)), ((), ())), preferred_element_type=F32)


def join3(x, rows):
    return x[:rows] + x[rows : 2 * rows] + x[2 * rows :]


def to_rows(x):
    return jnp.concatenate([x[:, 128 * c : 128 * c + 128] for c in range(4)], axis=0)


def to_grid(x):
    return jnp.concatenate([x[8 * c : 8 * c + 8] for c in range(4)], axis=1)


def onehot(mask):
    return jnp.where(mask, 1.0, 0.0).astype(BF16)


def primitives(u0, u1, u2, u3, u4):
    inverse = 1.0 / u0
    vx = u1 * inverse
    vy = u2 * inverse
    vz = u3 * inverse
    pressure = gas * (u4 - 0.5 * (u1 * vx + u2 * vy + u3 * vz))
    return inverse, vx, vy, vz, pressure


def start_all(copies):
    for copy in copies:
        copy.start()


def wait_all(copies):
    for copy in copies:
        copy.wait()


def begin_kernel(
    place,
    cell_hbm,
    zone_hbm,
    temps_hbm,
    spacing_hbm,
    flow_hbm,
    outgoing,
    rank_out,
    core_wall,
    cross_wall,
    wall_fields,
    pair_hbm,
    cross_hbm,
    cell,
    zone,
    temps,
    spacing,
    flow,
    sides,
    small_sem,
    in_sem,
    out_sem,
):
    even = place[0] % 2 == 0
    parity = place[1]
    small = [
        pltpu.make_async_copy(source, target, small_sem.at[index])
        for index, (source, target) in enumerate(
            (
                (cell_hbm, cell),
                (zone_hbm, zone),
                (temps_hbm.at[pl.ds(0, 8)], temps),
                (spacing_hbm, spacing),
            )
        )
    ]
    loads = [
        pltpu.make_async_copy(chunk_of(flow_hbm, c), chunk_of(flow, c), in_sem.at[c]) for c in range(4)
    ]
    start_all(small)
    start_all(loads)
    wait_all(small)
    cells = cell[...]
    tile = cells // 4096
    within = cells - tile * 4096
    hit = iota((32, 1024), 0) == tile
    ones = jnp.where(hit, 1.0, 0.0)
    stacked = jnp.concatenate([ones[:, 128 * k : 128 * k + 128] for k in range(8)], axis=0)
    inner = iota((128, 256), 0)
    outer = iota((128, 256), 1)
    ahead = onehot((inner < outer) | (outer >= 128))
    counts = dot_nn(stacked.astype(BF16), ahead)
    offset = jnp.zeros((32, 128), F32)
    ranks = []
    for k in range(8):
        part = slice(32 * k, 32 * k + 32)
        place = counts[part, :128] + offset
        ranks.append(jnp.sum(stacked[part] * place, axis=0, keepdims=True))
        offset = offset + counts[part, 128:]
    rank = jnp.concatenate(ranks, axis=1).astype(jnp.int32)
    rank_out[...] = rank
    slot = iota((32, 1024), 0) == rank
    first, second = temps[0:1], temps[1:2]
    fields = (within.astype(F32), (zone[...] + 1).astype(F32), first, second)
    pieces = [split3(value) for value in fields]
    rows = []
    for level in range(3):
        for piece in pieces:
            rows.append(jnp.where(slot, piece[level].astype(F32), 0.0).astype(BF16))
    sent = dot_nt(ones.astype(BF16), jnp.concatenate(rows, axis=0))
    outgoing[...] = sent[:, :128] + sent[:, 128:256] + sent[:, 256:]
    row = iota((8, 512), 0) // 2
    stores = []
    for c in range(4):
        loads[c].wait()

        def field(m, carry, c=c):
            for block in (2 * c, 2 * c + 1):
                high = jnp.zeros((8, 512), F32)
                low = jnp.zeros((8, 512), F32)
                for b in range(4):
                    plane = flow[m, block * 4 + b]
                    rolled_high = pltpu.roll(plane, (2 * b + 2) % 8, 0) if b != 3 else plane
                    rolled_low = pltpu.roll(plane, 2 * b, 0) if b else plane
                    high = jnp.where(row == b, rolled_high, high)
                    low = jnp.where(row == b, rolled_low, low)
                sides[0, m, block] = high
                sides[1, m, block] = low
            return carry

        lax.fori_loop(0, 5, field, 0)
        part = pl.ds(2 * c, 2)
        for index, (side, there) in enumerate(((parity, pair_hbm), (1 - parity, cross_hbm))):
            copy = pltpu.make_async_copy(sides.at[side, :, part], there.at[:, part], out_sem.at[index, c])
            copy.start()
            stores.append(copy)
    layers = [(flow[m, 30 + n], flow[m, n]) for m in range(5) for n in range(2)]
    layers += [(spacing[30 + n], spacing[n]) for n in range(2)]
    for index, (top, bottom) in enumerate(layers):
        core_wall[index] = jnp.where(even, top, bottom)
        cross_wall[index] = jnp.where(even, bottom, top)
    inverse, vx, vy, vz, pressure = primitives(*[flow[m, 0] for m in range(5)])
    film = 2.0 / spacing[0]
    temp = pressure * inverse + recovery * (vx * vx + vy * vy + vz * vz)
    total = spacing[0]
    for k in range(1, 32):
        total = total + spacing[k]
    for index, value in enumerate((film, temp, total)):
        core_wall[12 + index] = value
        cross_wall[12 + index] = value
        wall_fields[index] = value
    wait_all(stores)


def surface_kernel(
    place, conduct, rate, token, arrived, own, core, twin, cross, dense, sums, where_out
):
    wall = place[0]
    received = arrived[...]
    pieces = jnp.concatenate(split3(received), axis=0)
    lane = iota((128, 1024), 1) % 32
    line = iota((128, 1024), 0)
    source = iota((32, 1024), 0) == iota((32, 1024), 1) // 32
    flat = []
    for f in range(4):
        spread = join3(dot_nn(pieces, onehot(line == lane + 32 * f)), 32)
        flat.append(jnp.sum(jnp.where(source, spread, 0.0), axis=0, keepdims=True))
    where_out[...] = flat[0]
    cells = flat[0].astype(jnp.int32)
    block = ((cells % 512) // 128) * 8 + cells // 512
    block_hit = iota((32, 1024), 0) == block
    lane_hit = onehot(line == cells % 128)
    rows = [jnp.where(block_hit, flat[1], 0.0).astype(BF16)]
    for value in flat[2:]:
        for piece in split3(value):
            rows.append(jnp.where(block_hit, piece.astype(F32), 0.0).astype(BF16))
    grid = dot_nt(jnp.concatenate(rows, axis=0), lane_hit)
    zones = to_grid(grid[:32])
    surface = to_grid(join3(grid[32:128], 32))
    inner = to_grid(join3(grid[128:], 32))

    def from_bottom(f):
        return jnp.where(
            wall == 0,
            own[f],
            jnp.where(wall == 1, core[12 + f], jnp.where(wall == 2, twin[f], cross[12 + f])),
        )

    sums[0] = (own[2] + core[14]) + (twin[2] + cross[14])
    below = jnp.where(wall % 2 == 1, core[14], 0.0)
    sums[1] = below + jnp.where(wall >= 2, twin[2] + cross[14], 0.0)
    film = from_bottom(0)
    recover = from_bottom(1)
    cond = jnp.zeros((8, 512), F32)
    speed = jnp.zeros((8, 512), F32)
    for z in range(8):
        cond = jnp.where(zones == z + 1.0, conduct[z], cond)
        speed = jnp.where(zones == z + 1.0, rate[z], speed)
    base = film * recover + cond * inner
    for step in range(2):
        cube = surface * surface * surface
        surface = (base + 3.0 * radiation * cube * surface) / (film + cond + 4.0 * radiation * cube)
    recess = speed * jnp.exp(-activation / surface)
    taken = zones > 0.5
    dense[0] = jnp.where(taken, surface, 0.0)
    dense[1] = jnp.where(taken, recess, 0.0)


def return_kernel(where_in, dense, outgoing):
    cells = where_in[...].astype(jnp.int32)
    block = ((cells % 512) // 128) * 8 + cells // 512
    block_hit = iota((32, 1024), 0) == block
    line = iota((128, 1024), 0)
    lane_hit = onehot(line == cells % 128)
    pieces = jnp.concatenate(split3(to_rows(dense[0])), axis=0)
    spread = join3(dot_nn(pieces, lane_hit), 32)
    flat = jnp.sum(jnp.where(block_hit, spread, 0.0), axis=0, keepdims=True)
    source = iota((32, 1024), 0) == iota((32, 1024), 1) // 32
    rows = [jnp.where(source, piece.astype(F32), 0.0).astype(BF16) for piece in split3(flat)]
    slot = onehot(line == iota((128, 1024), 1) % 32)
    outgoing[...] = join3(dot_nt(jnp.concatenate(rows, axis=0), slot), 32)


def ablate_kernel(diffuse, token, cell, rank, zone, back, temps, out):
    pieces = jnp.concatenate(split3(back[...]), axis=0)
    slot = onehot(iota((128, 1024), 0) == rank[...])
    spread = join3(dot_nn(pieces, slot), 32)
    tile_hit = iota((32, 1024), 0) == cell[...] // 4096
    surface = jnp.sum(jnp.where(tile_hit, spread, 0.0), axis=0, keepdims=True)
    zones = zone[...]
    spread_rate = jnp.zeros((1, 1024), F32)
    for z in range(8):
        spread_rate = jnp.where(zones == z, diffuse[z], spread_rate)
    row = iota((64, 1024), 0)
    profile = jnp.where(row == 0, surface, temps[...])
    for step in range(2):
        before = pltpu.roll(profile, 1, 0)
        after = pltpu.roll(profile, 63, 0)
        after = jnp.where(row == 63, before, after)
        changed = profile + spread_rate * (after - 2.0 * profile + before)
        profile = jnp.where(row == 0, profile, changed)
    out[...] = profile


def chunk_of(ref, c):
    return ref.at[:, pl.ds(8 * c, 8)]


TWELFTH = time_step / 12.0


def side_kernel(token, flow_hbm, base_hbm, flow, base, in_sem, out_sem):
    loads = [
        pltpu.make_async_copy(chunk_of(flow_hbm, c), chunk_of(flow, c), in_sem.at[c]) for c in range(4)
    ]
    start_all(loads)
    row = iota((8, 512), 0)
    limits = (row != 7, row != 0, row < 6, row >= 2)

    def one_plane(k, carry):
        u = [flow[m, k] for m in range(5)]
        inverse, vx, vy, vz, pressure = primitives(*u)
        temp = pressure * inverse
        heat = u[4] + pressure
        shear = u[1] * vy
        flux_i = (u[1], u[1] * vx + pressure, shear, u[1] * vz, heat * vx)
        flux_j = (u[2], shear, u[2] * vy + pressure, u[2] * vz, heat * vy)
        smooth = (None, vx, vy, vz, temp)
        for m in range(5):
            result = u[m]
            w = smooth[m]
            if w is not None:
                amount = TWELFTH * diffusivity[m - 1]
                w16 = (16.0 * amount) * w
                w1 = amount * w
                result = result - (60.0 * amount) * w
            for axis, flux in ((0, flux_i[m]), (1, flux_j[m])):
                near = (8.0 * TWELFTH) * flux
                far = TWELFTH * flux
                if w is None:
                    sources = (near, -near, -far, far)
                else:
                    sources = (w16 + near, w16 - near, -w1 - far, far - w1)
                if axis == 0:
                    sources = [jnp.where(limit, value, 0.0) for limit, value in zip(limits, sources)]
                size = (8, 512)[axis]
                for shift, value in zip((1, size - 1, 2, size - 2), sources):
                    result = result + pltpu.roll(value, shift, axis)
            base[m, k] = result
        return carry

    stores = []
    for c in range(4):
        loads[c].wait()
        lax.fori_loop(8 * c, 8 * c + 8, one_plane, 0)
        copy = pltpu.make_async_copy(chunk_of(base, c), chunk_of(base_hbm, c), out_sem.at[c])
        copy.start()
        stores.append(copy)
    wait_all(stores)


def normal_flux(u3, density_x, density_y, vx, vy, vz, pressure, heat):
    return (u3, density_x * vz, density_y * vz, u3 * vz + pressure, heat * vz)


def normal_flux(u3, density_x, density_y, vx, vy, vz, pressure, heat):
    return (u3, density_x * vz, density_y * vz, u3 * vz + pressure, heat * vz)


def final_kernel(
    place,
    dense_hbm,
    dense_1_hbm,
    dense_2_hbm,
    dense_3_hbm,
    sums_hbm,
    core_hbm,
    cross_hbm,
    kinds_hbm,
    spacing_hbm,
    flow_hbm,
    base_hbm,
    far_hbm,
    pair_hbm,
    out_hbm,
    shift_hbm,
    dense,
    sums,
    walls,
    kinds,
    thick,
    flow,
    base,
    sides,
    fields,
    edges,
    run,
    shift,
    small_sem,
    flow_sem,
    base_sem,
    side_sem,
    out_sem,
    shift_sem,
):
    wall = place[0]
    parity = place[1]
    odd_wall = wall % 2
    small = [
        pltpu.make_async_copy(source, target, small_sem.at[index])
        for index, (source, target) in enumerate(
            (
                (dense_hbm, dense.at[0]),
                (dense_1_hbm, dense.at[1]),
                (dense_2_hbm, dense.at[2]),
                (dense_3_hbm, dense.at[3]),
                (sums_hbm, sums),
                (core_hbm.at[pl.ds(0, 12)], walls.at[1 - odd_wall]),
                (cross_hbm.at[pl.ds(0, 12)], walls.at[odd_wall]),
                (kinds_hbm, kinds),
                (spacing_hbm, thick.at[pl.ds(2, 32)]),
            )
        )
    ]
    start_all(small)

    def flow_load(c):
        return pltpu.make_async_copy(chunk_of(flow_hbm, c), chunk_of(flow, c), flow_sem.at[c])

    def other_loads(c):
        loads = [pltpu.make_async_copy(chunk_of(base_hbm, c), chunk_of(base, c), base_sem.at[c])]
        part = pl.ds(2 * c, 2)
        for index, (source, side) in enumerate(((pair_hbm, 1 - parity), (far_hbm, parity))):
            loads.append(
                pltpu.make_async_copy(source.at[:, part], sides.at[side, :, part], side_sem.at[index, c])
            )
        return loads

    flow_load(0).start()
    for c in range(4):
        if c < 3:
            flow_load(c + 1).start()
        start_all(other_loads(c))
    row = iota((8, 512), 0)
    odd = row % 2 == 1
    is_low = wall == 0
    is_high = wall == 3

    def store_fields(position, flux, smooth):
        for index, value in enumerate(flux + smooth):
            fields[index, position] = value

    def one_field(k, carry):
        u = [flow[m, k] for m in range(5)]
        inverse, vx, vy, vz, pressure = primitives(*u)
        flux = normal_flux(u[3], u[1], u[2], vx, vy, vz, pressure, u[4] + pressure)
        store_fields(k + 2, flux, (vx, vy, vz, pressure * inverse))
        return carry

    def prepare():
        wait_all(small)
        recess = (dense[0, 1] + dense[1, 1]) + (dense[2, 1] + dense[3, 1])
        total = sums[0]
        run[0] = sums[1]
        run[1] = total / (total + recess)
        run[2] = 1.0 / total
        run[3] = recess
        thick[0] = jnp.where(is_low, thick[2], walls[0, 10])
        thick[1] = jnp.where(is_low, thick[3], walls[0, 11])
        thick[34] = jnp.where(is_high, thick[32], walls[1, 10])
        thick[35] = jnp.where(is_high, thick[33], walls[1, 11])
        for layer in range(2):
            u = [jnp.where(is_high, far_values[m], walls[1, 2 * m + layer]) for m in range(5)]
            inverse, vx, vy, vz, pressure = primitives(*u)
            flux = normal_flux(u[3], u[1], u[2], vx, vy, vz, pressure, u[4] + pressure)
            store_fields(34 + layer, flux, (vx, vy, vz, pressure * inverse))
        kind = kinds[...]
        hot = (dense[0, 0] + dense[1, 0]) + (dense[2, 0] + dense[3, 0])
        cooled = 1.0 / hot
        slip = is_low & (kind == 1)
        blow = is_low & (kind == 2)
        sign = jnp.where(is_low, -1.0, 1.0)
        for layer in range(2):
            u = [jnp.where(is_low, flow[m, layer], walls[0, 2 * m + 1 - layer]) for m in range(5)]
            inverse, vx, vy, vz, pressure = primitives(*u)
            density = jnp.where(slip | jnp.logical_not(is_low), u[0], pressure * cooled)
            gx = jnp.where(slip, vx, sign * vx)
            gy = jnp.where(slip, vy, sign * vy)
            gz = jnp.where(blow, 2.0 * recess, 0.0) + sign * vz
            heat = pressure * (1.0 / gas + 1.0) + 0.5 * density * (gx * gx + gy * gy + gz * gz)
            flux = normal_flux(density * gz, density * gx, density * gy, gx, gy, gz, pressure, heat)
            store_fields(1 - layer, flux, (gx, gy, gz, pressure / density))

    def one_block(block, carry):
        for side, near_sign in ((0, 1.0), (1, -1.0)):
            u = [sides[side, m, block] for m in range(5)]
            inverse, vx, vy, vz, pressure = primitives(*u)
            flux = (u[1], u[1] * vx + pressure, u[1] * vy, u[1] * vz, (u[4] + pressure) * vx)
            smooth = (None, vx, vy, vz, pressure * inverse)
            for m in range(5):
                near = (8.0 * TWELFTH * near_sign) * flux[m]
                far = (-TWELFTH * near_sign) * flux[m]
                if smooth[m] is not None:
                    amount = TWELFTH * diffusivity[m - 1]
                    near = near + (16.0 * amount) * smooth[m]
                    far = far - amount * smooth[m]
                if near_sign > 0:
                    moved = jnp.where(odd, 0.0, pltpu.roll(near, 7, 0))
                else:
                    moved = jnp.where(odd, pltpu.roll(near, 1, 0), 0.0)
                edges[side, m] = far + moved
        for b in range(4):
            k = block * 4 + b
            width = thick[k + 2]
            center = run[0] + 0.5 * width
            run[0] = run[0] + width
            normal = center * run[2]
            shift[k] = run[3] * (normal - 1.0)
            stretch = 7.0 * width + 3.0 * (thick[k + 1] + thick[k + 3]) - 0.5 * (thick[k] + thick[k + 4])
            factor = run[1] * (12.0 / stretch)
            damp = (time_step * sponge_rate) * (normal * normal)
            slope_scale = -TWELFTH * factor
            curve_scale = TWELFTH * (factor * factor)
            for m in range(5):
                f = [fields[m, k + o] for o in (0, 1, 3, 4)]
                slope = 8.0 * (f[2] - f[1]) - (f[3] - f[0])
                value = base[m, k] + slope_scale * slope - damp * (flow[m, k] - far_values[m])
                if m:
                    g = [fields[m + 4, k + o] for o in range(5)]
                    curve = 16.0 * (g[1] + g[3]) - (g[0] + g[4]) - 30.0 * g[2]
                    value = value + (curve_scale * diffusivity[m - 1]) * curve
                low_edge = pltpu.roll(edges[0, m], 8 - 2 * b, 0) if b else edges[0, m]
                high_edge = pltpu.roll(edges[1, m], (6 - 2 * b) % 8, 0) if b != 3 else edges[1, m]
                base[m, k] = value + jnp.where(row < 2, low_edge, jnp.where(row >= 6, high_edge, 0.0))
        return carry

    def stores(c):
        rows = pl.ds(8 * c, 8)
        return [
            pltpu.make_async_copy(chunk_of(base, c), chunk_of(out_hbm, c), out_sem.at[c]),
            pltpu.make_async_copy(shift.at[rows], shift_hbm.at[rows], shift_sem.at[c]),
        ]

    def one_chunk(c, carry):
        @pl.when(c < 4)
        def fill():
            flow_load(c).wait()
            lax.fori_loop(8 * c, 8 * c + 8, one_field, 0)

        @pl.when(c == 0)
        def begin():
            prepare()

        @pl.when(c > 0)
        def finish():
            wait_all(other_loads(c - 1))
            lax.fori_loop(2 * c - 2, 2 * c, one_block, 0)
            start_all(stores(c - 1))

        return carry

    lax.fori_loop(0, 5, one_chunk, 0)
    for c in range(4):
        wait_all(stores(c))


def whole(shape):
    return pl.BlockSpec(shape, lambda *_: (0,) * len(shape))


SCALARS = pl.BlockSpec(memory_space=pltpu.SMEM)
ANY = pl.BlockSpec(memory_space=pl.ANY)
VMEM = pl.BlockSpec(memory_space=pltpu.VMEM)


def params():
    return pltpu.CompilerParams(vmem_limit_bytes=62 * 1024 * 1024)


def cost():
    return pl.CostEstimate(flops=1000, transcendentals=0, bytes_accessed=1000)


def struct(*shape, dtype=F32):
    return jax.ShapeDtypeStruct(shape, dtype)


def call(kernel, name, out_shape, **options):
    return pl.pallas_call(
        kernel, out_shape=out_shape, name=name, compiler_params=params(), cost_estimate=cost(), **options
    )


def scratch(*shape):
    return pltpu.VMEM(shape, F32)


def copies(*shape):
    return pltpu.SemaphoreType.DMA(shape)


def shards(flow_state, spacing, bc_kind, cell_of, zone_id, abl_temp, conduct, diffuse, rate):
    surf_count = lax.axis_size("surf")
    place = jnp.stack([lax.axis_index("wall"), lax.axis_index("surf") % 2]).astype(jnp.int32)
    cells = cell_of.reshape(1, 1024)
    zones = zone_id.reshape(1, 1024)

    def swap(value, axis, partner):
        return lax.ppermute(value, axis, [(i, partner(i)) for i in range(lax.axis_size(axis))])

    outgoing, rank, core_wall, cross_wall, wall_fields, pair_side, cross_side = call(
        begin_kernel,
        "begin",
        (
            struct(32, 128),
            struct(1, 1024, dtype=jnp.int32),
            struct(15, 8, 512),
            struct(15, 8, 512),
            struct(3, 8, 512),
            struct(5, 8, 8, 512),
            struct(5, 8, 8, 512),
        ),
        in_specs=[SCALARS] + [ANY] * 5,
        out_specs=(VMEM,) * 5 + (ANY,) * 2,
        scratch_shapes=[
            pltpu.VMEM((1, 1024), jnp.int32),
            pltpu.VMEM((1, 1024), jnp.int32),
            scratch(8, 1024),
            scratch(32, 8, 512),
            scratch(5, 32, 8, 512),
            scratch(2, 5, 8, 8, 512),
            copies(4),
            copies(4),
            copies(2, 4),
        ],
    )(place, cells, zones, abl_temp, spacing, flow_state)
    arrived = lax.all_to_all(outgoing, "surf", split_axis=0, concat_axis=0, tiled=True)
    cross = swap(cross_wall, "wall", lambda i: i ^ 3)
    twin = swap(wall_fields, "wall", lambda i: i ^ 2)
    core = swap(core_wall, "wall", lambda i: i ^ 1)
    far = swap(cross_side, "surf", lambda i: (i - 1 + 2 * (i % 2)) % surf_count)
    pair = swap(pair_side, "surf", lambda i: i ^ 1)
    base = call(
        side_kernel,
        "side",
        struct(5, 32, 8, 512),
        in_specs=[ANY, ANY],
        out_specs=ANY,
        scratch_shapes=[scratch(5, 32, 8, 512), scratch(5, 32, 8, 512), copies(4), copies(4)],
    )(rank, flow_state)
    dense, sums, where_cells = call(
        surface_kernel,
        "surface",
        (struct(2, 8, 512), struct(2, 8, 512), struct(1, 1024)),
        in_specs=[SCALARS] * 3 + [ANY] + [VMEM] * 5,
    )(place, conduct, rate, base, arrived, wall_fields, core, twin, cross)
    dense_1, dense_2, dense_3 = (swap(dense, "wall", lambda i, by=by: i ^ by) for by in (1, 2, 3))
    returned = call(return_kernel, "answer", struct(32, 128))(where_cells, dense)
    back = lax.all_to_all(returned, "surf", split_axis=0, concat_axis=0, tiled=True)
    state_next, node_shift = call(
        final_kernel,
        "final",
        (struct(5, 32, 8, 512), struct(32, 8, 512)),
        in_specs=[SCALARS] + [ANY] * 13,
        out_specs=(ANY, ANY),
        scratch_shapes=[
            scratch(4, 2, 8, 512),
            scratch(2, 8, 512),
            scratch(2, 12, 8, 512),
            pltpu.VMEM((8, 512), jnp.int32),
            scratch(36, 8, 512),
            scratch(5, 32, 8, 512),
            scratch(5, 32, 8, 512),
            scratch(2, 5, 8, 8, 512),
            scratch(9, 36, 8, 512),
            scratch(2, 5, 8, 512),
            scratch(4, 8, 512),
            scratch(32, 8, 512),
            copies(9),
            copies(4),
            copies(4),
            copies(2, 4),
            copies(4),
            copies(4),
        ],
    )(
        place,
        dense,
        dense_1,
        dense_2,
        dense_3,
        sums,
        core,
        cross,
        bc_kind,
        spacing,
        flow_state,
        base,
        far,
        pair,
    )
    ablator_next = call(
        ablate_kernel,
        "ablate",
        struct(64, 1024),
        in_specs=[SCALARS, ANY] + [VMEM] * 5,
    )(diffuse, node_shift, cells, rank, zones, back, abl_temp)
    return (state_next, node_shift, ablator_next)


def solution(mesh):
    in_specs = (
        P(None, "wall", "surf", None),
        P("wall", "surf", None),
        P("surf", None),
        P(("surf", "wall")),
        P(("surf", "wall")),
        P(None, ("surf", "wall")),
        P(),
        P(),
        P(),
    )
    out_specs = (P(None, "wall", "surf", None), P("wall", "surf", None), P(None, ("surf", "wall")))
    return jax.shard_map(shards, mesh=mesh, in_specs=in_specs, out_specs=out_specs, check_vma=False)
```

```python
import functools
import jax
import jax.numpy as jnp
from jax import lax
from jax.experimental import pallas as pl
from jax.experimental.pallas import tpu as pltpu
from jax.sharding import PartitionSpec as P

gas = 0.4
time_step = 0.15
viscosity = 0.05
conduction = 0.07
sponge_rate = 0.5
activation = 2.0
radiation = 0.8
recovery = 0.2
far_values = (1.0, 0.5, 0.0, 0.0, 2.625)
diffusivity = (viscosity, viscosity, viscosity, conduction)

F32 = jnp.float32
BF16 = jnp.bfloat16


def iota(shape, axis):
    return lax.broadcasted_iota(jnp.int32, shape, axis)


def split3(x):
    high = x.astype(BF16)
    rest = x - high.astype(F32)
    middle = rest.astype(BF16)
    low = (rest - middle.astype(F32)).astype(BF16)
    return high, middle, low


def dot_nn(a, b):
    return lax.dot_general(a, b, (((1,), (0,)), ((), ())), preferred_element_type=F32)


def dot_nt(a, b):
    return lax.dot_general(a, b, (((1,), (1,)), ((), ())), preferred_element_type=F32)


def join3(x, rows):
    return x[:rows] + x[rows : 2 * rows] + x[2 * rows :]


def to_rows(x):
    return jnp.concatenate([x[:, 128 * c : 128 * c + 128] for c in range(4)], axis=0)


def to_grid(x):
    return jnp.concatenate([x[8 * c : 8 * c + 8] for c in range(4)], axis=1)


def onehot(mask):
    return jnp.where(mask, 1.0, 0.0).astype(BF16)


def primitives(u0, u1, u2, u3, u4):
    inverse = 1.0 / u0
    vx = u1 * inverse
    vy = u2 * inverse
    vz = u3 * inverse
    pressure = gas * (u4 - 0.5 * (u1 * vx + u2 * vy + u3 * vz))
    return inverse, vx, vy, vz, pressure


def start_all(copies):
    for copy in copies:
        copy.start()


def wait_all(copies):
    for copy in copies:
        copy.wait()


def begin_kernel(
    cell_hbm,
    zone_hbm,
    temps_hbm,
    spacing_hbm,
    flow_hbm,
    outgoing,
    rank_out,
    core_wall,
    cross_layers,
    wall_fields,
    pair_hbm,
    cross_hbm,
    cell,
    zone,
    temps,
    spacing,
    flow,
    sides,
    small_sem,
    in_sem,
    out_sem,
):
    even = lax.axis_index("wall") % 2 == 0
    parity = lax.axis_index("surf") % 2
    small = [
        pltpu.make_async_copy(source, target, small_sem.at[index])
        for index, (source, target) in enumerate(
            (
                (cell_hbm, cell),
                (zone_hbm, zone),
                (temps_hbm.at[pl.ds(0, 8)], temps),
                (spacing_hbm, spacing),
            )
        )
    ]
    loads = [
        pltpu.make_async_copy(chunk_of(flow_hbm, c), chunk_of(flow, c), in_sem.at[c]) for c in range(4)
    ]
    start_all(small)
    start_all(loads)
    wait_all(small)
    cells = cell[...]
    tile = cells // 4096
    within = cells - tile * 4096
    hit = iota((32, 1024), 0) == tile
    ones = jnp.where(hit, 1.0, 0.0)
    stacked = jnp.concatenate([ones[:, 128 * k : 128 * k + 128] for k in range(8)], axis=0)
    inner = iota((128, 256), 0)
    outer = iota((128, 256), 1)
    ahead = onehot((inner < outer) | (outer >= 128))
    counts = dot_nn(stacked.astype(BF16), ahead)
    offset = jnp.zeros((32, 128), F32)
    ranks = []
    for k in range(8):
        part = slice(32 * k, 32 * k + 32)
        place = counts[part, :128] + offset
        ranks.append(jnp.sum(stacked[part] * place, axis=0, keepdims=True))
        offset = offset + counts[part, 128:]
    rank = jnp.concatenate(ranks, axis=1).astype(jnp.int32)
    rank_out[...] = rank
    slot = iota((32, 1024), 0) == rank
    first, second = temps[0:1], temps[1:2]
    fields = (within.astype(F32), (zone[...] + 1).astype(F32), first, second)
    pieces = [split3(value) for value in fields]
    rows = []
    for level in range(3):
        for piece in pieces:
            rows.append(jnp.where(slot, piece[level].astype(F32), 0.0).astype(BF16))
    sent = dot_nt(ones.astype(BF16), jnp.concatenate(rows, axis=0))
    outgoing[...] = sent[:, :128] + sent[:, 128:256] + sent[:, 256:]
    row = iota((8, 512), 0) // 2
    stores = []
    for c in range(4):
        loads[c].wait()

        def field(m, carry, c=c):
            for block in (2 * c, 2 * c + 1):
                high = jnp.zeros((8, 512), F32)
                low = jnp.zeros((8, 512), F32)
                for b in range(4):
                    plane = flow[m, block * 4 + b]
                    rolled_high = pltpu.roll(plane, (2 * b + 2) % 8, 0) if b != 3 else plane
                    rolled_low = pltpu.roll(plane, 2 * b, 0) if b else plane
                    high = jnp.where(row == b, rolled_high, high)
                    low = jnp.where(row == b, rolled_low, low)
                sides[0, m, block] = high
                sides[1, m, block] = low
            return carry

        lax.fori_loop(0, 5, field, 0)
        part = pl.ds(2 * c, 2)
        for index, (side, there) in enumerate(((parity, pair_hbm), (1 - parity, cross_hbm))):
            copy = pltpu.make_async_copy(sides.at[side, :, part], there.at[:, part], out_sem.at[index, c])
            copy.start()
            stores.append(copy)
    layers = [(flow[m, 30 + n], flow[m, n]) for m in range(5) for n in range(2)]
    layers += [(spacing[30 + n], spacing[n]) for n in range(2)]
    for index, (top, bottom) in enumerate(layers):
        core_wall[index] = jnp.where(even, top, bottom)
        cross_layers[index] = jnp.where(even, bottom, top)
    inverse, vx, vy, vz, pressure = primitives(*[flow[m, 0] for m in range(5)])
    film = 2.0 / spacing[0]
    temp = pressure * inverse + recovery * (vx * vx + vy * vy + vz * vz)
    total = spacing[0]
    for k in range(1, 32):
        total = total + spacing[k]
    for index, value in enumerate((film, temp, total)):
        core_wall[12 + index] = value
        wall_fields[index] = value
    wait_all(stores)


def surface_kernel(
    conduct, rate, token, arrived, own, core, twin, cross, dense, sums, where_out
):
    wall = lax.axis_index("wall")
    received = arrived[...]
    pieces = jnp.concatenate(split3(received), axis=0)
    lane = iota((128, 1024), 1) % 32
    line = iota((128, 1024), 0)
    source = iota((32, 1024), 0) == iota((32, 1024), 1) // 32
    flat = []
    for f in range(4):
        spread = join3(dot_nn(pieces, onehot(line == lane + 32 * f)), 32)
        flat.append(jnp.sum(jnp.where(source, spread, 0.0), axis=0, keepdims=True))
    where_out[...] = flat[0]
    cells = flat[0].astype(jnp.int32)
    block = ((cells % 512) // 128) * 8 + cells // 512
    block_hit = iota((32, 1024), 0) == block
    lane_hit = onehot(line == cells % 128)
    rows = [jnp.where(block_hit, flat[1], 0.0).astype(BF16)]
    for value in flat[2:]:
        for piece in split3(value):
            rows.append(jnp.where(block_hit, piece.astype(F32), 0.0).astype(BF16))
    grid = dot_nt(jnp.concatenate(rows, axis=0), lane_hit)
    zones = to_grid(grid[:32])
    surface = to_grid(join3(grid[32:128], 32))
    inner = to_grid(join3(grid[128:], 32))

    def from_bottom(f):
        return jnp.where(
            wall == 0,
            own[f],
            jnp.where(wall == 1, core[12 + f], jnp.where(wall == 2, twin[f], cross[f])),
        )

    sums[0] = (own[2] + core[14]) + (twin[2] + cross[2])
    below = jnp.where(wall % 2 == 1, core[14], 0.0)
    sums[1] = below + jnp.where(wall >= 2, twin[2] + cross[2], 0.0)
    film = from_bottom(0)
    recover = from_bottom(1)
    cond = jnp.zeros((8, 512), F32)
    speed = jnp.zeros((8, 512), F32)
    for z in range(8):
        cond = jnp.where(zones == z + 1.0, conduct[z], cond)
        speed = jnp.where(zones == z + 1.0, rate[z], speed)
    base = film * recover + cond * inner
    for step in range(2):
        cube = surface * surface * surface
        surface = (base + 3.0 * radiation * cube * surface) / (film + cond + 4.0 * radiation * cube)
    recess = speed * jnp.exp(-activation / surface)
    taken = zones > 0.5
    dense[0] = jnp.where(taken, surface, 0.0)
    dense[1] = jnp.where(taken, recess, 0.0)


def return_kernel(where_in, dense, outgoing):
    cells = where_in[...].astype(jnp.int32)
    block = ((cells % 512) // 128) * 8 + cells // 512
    block_hit = iota((32, 1024), 0) == block
    line = iota((128, 1024), 0)
    lane_hit = onehot(line == cells % 128)
    pieces = jnp.concatenate(split3(to_rows(dense[0])), axis=0)
    spread = join3(dot_nn(pieces, lane_hit), 32)
    flat = jnp.sum(jnp.where(block_hit, spread, 0.0), axis=0, keepdims=True)
    source = iota((32, 1024), 0) == iota((32, 1024), 1) // 32
    rows = [jnp.where(source, piece.astype(F32), 0.0).astype(BF16) for piece in split3(flat)]
    slot = onehot(line == iota((128, 1024), 1) % 32)
    outgoing[...] = join3(dot_nt(jnp.concatenate(rows, axis=0), slot), 32)


def ablate_kernel(diffuse, token, cell, rank, zone, back, temps, out):
    pieces = jnp.concatenate(split3(back[...]), axis=0)
    slot = onehot(iota((128, 1024), 0) == rank[...])
    spread = join3(dot_nn(pieces, slot), 32)
    tile_hit = iota((32, 1024), 0) == cell[...] // 4096
    surface = jnp.sum(jnp.where(tile_hit, spread, 0.0), axis=0, keepdims=True)
    zones = zone[...]
    spread_rate = jnp.zeros((1, 1024), F32)
    for z in range(8):
        spread_rate = jnp.where(zones == z, diffuse[z], spread_rate)
    row = iota((64, 1024), 0)
    profile = jnp.where(row == 0, surface, temps[...])
    for step in range(2):
        before = pltpu.roll(profile, 1, 0)
        after = pltpu.roll(profile, 63, 0)
        after = jnp.where(row == 63, before, after)
        changed = profile + spread_rate * (after - 2.0 * profile + before)
        profile = jnp.where(row == 0, profile, changed)
    out[...] = profile


def chunk_of(ref, c):
    return ref.at[:, pl.ds(8 * c, 8)]


TWELFTH = time_step / 12.0


def side_kernel(token, flow_hbm, base_hbm, done, flow, base, in_sem, out_sem):
    done[...] = jnp.zeros_like(done)
    loads = [
        pltpu.make_async_copy(chunk_of(flow_hbm, c), chunk_of(flow, c), in_sem.at[c]) for c in range(4)
    ]
    start_all(loads)
    row = iota((8, 512), 0)
    limits = (row != 7, row != 0, row < 6, row >= 2)

    def one_plane(k, carry):
        u = [flow[m, k] for m in range(5)]
        inverse, vx, vy, vz, pressure = primitives(*u)
        temp = pressure * inverse
        heat = u[4] + pressure
        shear = u[1] * vy
        flux_i = (u[1], u[1] * vx + pressure, shear, u[1] * vz, heat * vx)
        flux_j = (u[2], shear, u[2] * vy + pressure, u[2] * vz, heat * vy)
        smooth = (None, vx, vy, vz, temp)
        for m in range(5):
            result = u[m]
            w = smooth[m]
            if w is not None:
                amount = TWELFTH * diffusivity[m - 1]
                w16 = (16.0 * amount) * w
                w1 = amount * w
                result = result - (60.0 * amount) * w
            for axis, flux in ((0, flux_i[m]), (1, flux_j[m])):
                near = (8.0 * TWELFTH) * flux
                far = TWELFTH * flux
                if w is None:
                    sources = (near, -near, -far, far)
                else:
                    sources = (w16 + near, w16 - near, -w1 - far, far - w1)
                if axis == 0:
                    sources = [jnp.where(limit, value, 0.0) for limit, value in zip(limits, sources)]
                size = (8, 512)[axis]
                for shift, value in zip((1, size - 1, 2, size - 2), sources):
                    result = result + pltpu.roll(value, shift, axis)
            base[m, k] = result
        return carry

    stores = []
    for c in range(4):
        loads[c].wait()
        lax.fori_loop(8 * c, 8 * c + 8, one_plane, 0)
        copy = pltpu.make_async_copy(chunk_of(base, c), chunk_of(base_hbm, c), out_sem.at[c])
        copy.start()
        stores.append(copy)
    wait_all(stores)


def normal_flux(u3, density_x, density_y, vx, vy, vz, pressure, heat):
    return (u3, density_x * vz, density_y * vz, u3 * vz + pressure, heat * vz)


def normal_flux(u3, density_x, density_y, vx, vy, vz, pressure, heat):
    return (u3, density_x * vz, density_y * vz, u3 * vz + pressure, heat * vz)


def final_kernel(
    dense_hbm,
    dense_1_hbm,
    dense_2_hbm,
    dense_3_hbm,
    sums_hbm,
    core_hbm,
    cross_hbm,
    kinds_hbm,
    spacing_hbm,
    flow_hbm,
    base_hbm,
    far_hbm,
    pair_hbm,
    out_hbm,
    shift_hbm,
    done,
    dense,
    sums,
    walls,
    kinds,
    thick,
    flow,
    base,
    sides,
    fields,
    edges,
    run,
    shift,
    small_sem,
    flow_sem,
    base_sem,
    side_sem,
    out_sem,
    shift_sem,
):
    wall = lax.axis_index("wall")
    parity = lax.axis_index("surf") % 2
    odd_wall = wall % 2
    small = [
        pltpu.make_async_copy(source, target, small_sem.at[index])
        for index, (source, target) in enumerate(
            (
                (dense_hbm, dense.at[0]),
                (dense_1_hbm, dense.at[1]),
                (dense_2_hbm, dense.at[2]),
                (dense_3_hbm, dense.at[3]),
                (sums_hbm, sums),
                (core_hbm.at[pl.ds(0, 12)], walls.at[1 - odd_wall]),
                (cross_hbm, walls.at[odd_wall]),
                (kinds_hbm, kinds),
                (spacing_hbm, thick.at[pl.ds(2, 32)]),
            )
        )
    ]
    done[...] = jnp.zeros_like(done)
    start_all(small)

    def flow_load(c):
        return pltpu.make_async_copy(chunk_of(flow_hbm, c), chunk_of(flow, c), flow_sem.at[c])

    def other_loads(c):
        loads = [pltpu.make_async_copy(chunk_of(base_hbm, c), chunk_of(base, c), base_sem.at[c])]
        part = pl.ds(2 * c, 2)
        for index, (source, side) in enumerate(((pair_hbm, 1 - parity), (far_hbm, parity))):
            loads.append(
                pltpu.make_async_copy(source.at[:, part], sides.at[side, :, part], side_sem.at[index, c])
            )
        return loads

    flow_load(0).start()
    for c in range(4):
        if c < 3:
            flow_load(c + 1).start()
        start_all(other_loads(c))
    row = iota((8, 512), 0)
    odd = row % 2 == 1
    is_low = wall == 0
    is_high = wall == 3

    def store_fields(position, flux, smooth):
        for index, value in enumerate(flux + smooth):
            fields[index, position] = value

    def one_field(k, carry):
        u = [flow[m, k] for m in range(5)]
        inverse, vx, vy, vz, pressure = primitives(*u)
        flux = normal_flux(u[3], u[1], u[2], vx, vy, vz, pressure, u[4] + pressure)
        store_fields(k + 2, flux, (vx, vy, vz, pressure * inverse))
        return carry

    def prepare():
        wait_all(small)
        recess = (dense[0, 1] + dense[1, 1]) + (dense[2, 1] + dense[3, 1])
        total = sums[0]
        run[0] = sums[1]
        run[1] = total / (total + recess)
        run[2] = 1.0 / total
        run[3] = recess
        thick[0] = jnp.where(is_low, thick[2], walls[0, 10])
        thick[1] = jnp.where(is_low, thick[3], walls[0, 11])
        thick[34] = jnp.where(is_high, thick[32], walls[1, 10])
        thick[35] = jnp.where(is_high, thick[33], walls[1, 11])
        for layer in range(2):
            u = [jnp.where(is_high, far_values[m], walls[1, 2 * m + layer]) for m in range(5)]
            inverse, vx, vy, vz, pressure = primitives(*u)
            flux = normal_flux(u[3], u[1], u[2], vx, vy, vz, pressure, u[4] + pressure)
            store_fields(34 + layer, flux, (vx, vy, vz, pressure * inverse))
        kind = kinds[...]
        hot = (dense[0, 0] + dense[1, 0]) + (dense[2, 0] + dense[3, 0])
        cooled = 1.0 / hot
        slip = is_low & (kind == 1)
        blow = is_low & (kind == 2)
        sign = jnp.where(is_low, -1.0, 1.0)
        for layer in range(2):
            u = [jnp.where(is_low, flow[m, layer], walls[0, 2 * m + 1 - layer]) for m in range(5)]
            inverse, vx, vy, vz, pressure = primitives(*u)
            density = jnp.where(slip | jnp.logical_not(is_low), u[0], pressure * cooled)
            gx = jnp.where(slip, vx, sign * vx)
            gy = jnp.where(slip, vy, sign * vy)
            gz = jnp.where(blow, 2.0 * recess, 0.0) + sign * vz
            heat = pressure * (1.0 / gas + 1.0) + 0.5 * density * (gx * gx + gy * gy + gz * gz)
            flux = normal_flux(density * gz, density * gx, density * gy, gx, gy, gz, pressure, heat)
            store_fields(1 - layer, flux, (gx, gy, gz, pressure / density))

    def one_block(block, carry):
        for side, near_sign in ((0, 1.0), (1, -1.0)):
            u = [sides[side, m, block] for m in range(5)]
            inverse, vx, vy, vz, pressure = primitives(*u)
            flux = (u[1], u[1] * vx + pressure, u[1] * vy, u[1] * vz, (u[4] + pressure) * vx)
            smooth = (None, vx, vy, vz, pressure * inverse)
            for m in range(5):
                near = (8.0 * TWELFTH * near_sign) * flux[m]
                far = (-TWELFTH * near_sign) * flux[m]
                if smooth[m] is not None:
                    amount = TWELFTH * diffusivity[m - 1]
                    near = near + (16.0 * amount) * smooth[m]
                    far = far - amount * smooth[m]
                if near_sign > 0:
                    moved = jnp.where(odd, 0.0, pltpu.roll(near, 7, 0))
                else:
                    moved = jnp.where(odd, pltpu.roll(near, 1, 0), 0.0)
                edges[side, m] = far + moved
        for b in range(4):
            k = block * 4 + b
            width = thick[k + 2]
            center = run[0] + 0.5 * width
            run[0] = run[0] + width
            normal = center * run[2]
            shift[k] = run[3] * (normal - 1.0)
            stretch = 7.0 * width + 3.0 * (thick[k + 1] + thick[k + 3]) - 0.5 * (thick[k] + thick[k + 4])
            factor = run[1] * (12.0 / stretch)
            damp = (time_step * sponge_rate) * (normal * normal)
            slope_scale = -TWELFTH * factor
            curve_scale = TWELFTH * (factor * factor)
            for m in range(5):
                f = [fields[m, k + o] for o in (0, 1, 3, 4)]
                slope = 8.0 * (f[2] - f[1]) - (f[3] - f[0])
                value = base[m, k] + slope_scale * slope - damp * (flow[m, k] - far_values[m])
                if m:
                    g = [fields[m + 4, k + o] for o in range(5)]
                    curve = 16.0 * (g[1] + g[3]) - (g[0] + g[4]) - 30.0 * g[2]
                    value = value + (curve_scale * diffusivity[m - 1]) * curve
                low_edge = pltpu.roll(edges[0, m], 8 - 2 * b, 0) if b else edges[0, m]
                high_edge = pltpu.roll(edges[1, m], (6 - 2 * b) % 8, 0) if b != 3 else edges[1, m]
                base[m, k] = value + jnp.where(row < 2, low_edge, jnp.where(row >= 6, high_edge, 0.0))
        return carry

    def stores(c):
        rows = pl.ds(8 * c, 8)
        return [
            pltpu.make_async_copy(chunk_of(base, c), chunk_of(out_hbm, c), out_sem.at[c]),
            pltpu.make_async_copy(shift.at[rows], shift_hbm.at[rows], shift_sem.at[c]),
        ]

    def one_chunk(c, carry):
        @pl.when(c < 4)
        def fill():
            flow_load(c).wait()
            lax.fori_loop(8 * c, 8 * c + 8, one_field, 0)

        @pl.when(c == 0)
        def begin():
            prepare()

        @pl.when(c > 0)
        def finish():
            wait_all(other_loads(c - 1))
            lax.fori_loop(2 * c - 2, 2 * c, one_block, 0)
            start_all(stores(c - 1))

        return carry

    lax.fori_loop(0, 5, one_chunk, 0)
    for c in range(4):
        wait_all(stores(c))


def whole(shape):
    return pl.BlockSpec(shape, lambda *_: (0,) * len(shape))


SCALARS = pl.BlockSpec(memory_space=pltpu.SMEM)
ANY = pl.BlockSpec(memory_space=pl.ANY)
HBM = pl.BlockSpec(memory_space=pltpu.HBM)
VMEM = pl.BlockSpec(memory_space=pltpu.VMEM)


def params(grant):
    return pltpu.CompilerParams(vmem_limit_bytes=grant * 1024 * 1024)


def cost():
    return pl.CostEstimate(flops=1000, transcendentals=0, bytes_accessed=1000)


def struct(*shape, dtype=F32):
    return jax.ShapeDtypeStruct(shape, dtype)


def call(kernel, name, out_shape, grant=62, **options):
    return pl.pallas_call(
        kernel,
        out_shape=out_shape,
        name=name,
        compiler_params=params(grant),
        cost_estimate=cost(),
        **options,
    )


def scratch(*shape):
    return pltpu.VMEM(shape, F32)


def copies(*shape):
    return pltpu.SemaphoreType.DMA(shape)


def shards(flow_state, spacing, bc_kind, cell_of, zone_id, abl_temp, conduct, diffuse, rate):
    surf_count = lax.axis_size("surf")
    cells = cell_of.reshape(1, 1024)
    zones = zone_id.reshape(1, 1024)

    def swap(value, axis, partner):
        return lax.ppermute(value, axis, [(i, partner(i)) for i in range(lax.axis_size(axis))])

    outgoing, rank, core_wall, cross_layers, wall_fields, pair_side, cross_side = call(
        begin_kernel,
        "begin",
        (
            struct(32, 128),
            struct(1, 1024, dtype=jnp.int32),
            struct(15, 8, 512),
            struct(12, 8, 512),
            struct(3, 8, 512),
            struct(5, 8, 8, 512),
            struct(5, 8, 8, 512),
        ),
        in_specs=[ANY] * 5,
        out_specs=(VMEM,) * 5 + (ANY,) * 2,
        scratch_shapes=[
            pltpu.VMEM((1, 1024), jnp.int32),
            pltpu.VMEM((1, 1024), jnp.int32),
            scratch(8, 1024),
            scratch(32, 8, 512),
            scratch(5, 32, 8, 512),
            scratch(2, 5, 8, 8, 512),
            copies(4),
            copies(4),
            copies(2, 4),
        ],
    )(cells, zones, abl_temp, spacing, flow_state)
    arrived = lax.all_to_all(outgoing, "surf", split_axis=0, concat_axis=0, tiled=True)
    cross = swap(wall_fields, "wall", lambda i: i ^ 3)
    twin = swap(wall_fields, "wall", lambda i: i ^ 2)
    core = swap(core_wall, "wall", lambda i: i ^ 1)
    far = swap(cross_side, "surf", lambda i: (i - 1 + 2 * (i % 2)) % surf_count)
    pair = swap(pair_side, "surf", lambda i: i ^ 1)
    base, side_done = call(
        side_kernel,
        "side",
        (struct(5, 32, 8, 512), struct(8, 128)),
        in_specs=[ANY, HBM],
        out_specs=(HBM, VMEM),
        scratch_shapes=[scratch(5, 32, 8, 512), scratch(5, 32, 8, 512), copies(4), copies(4)],
    )(rank, flow_state)
    dense, sums, where_cells = call(
        surface_kernel,
        "surface",
        (struct(2, 8, 512), struct(2, 8, 512), struct(1, 1024)),
        grant=32,
        in_specs=[SCALARS] * 2 + [ANY] + [VMEM] * 5,
    )(conduct, rate, side_done, arrived, wall_fields, core, twin, cross)
    cross_layers, where_cells = lax.optimization_barrier((cross_layers, where_cells))
    layers = lax.ppermute(cross_layers, "wall", [(1, 2), (2, 1)])
    dense_1, dense_2, dense_3 = (swap(dense, "wall", lambda i, by=by: i ^ by) for by in (1, 2, 3))
    returned = call(return_kernel, "answer", struct(32, 128), grant=32)(where_cells, dense)
    back = lax.all_to_all(returned, "surf", split_axis=0, concat_axis=0, tiled=True)
    state_next, node_shift, final_done = call(
        final_kernel,
        "final",
        (struct(5, 32, 8, 512), struct(32, 8, 512), struct(8, 128)),
        grant=52,
        in_specs=[ANY] * 8 + [HBM] * 5,
        out_specs=(HBM, HBM, VMEM),
        scratch_shapes=[
            scratch(4, 2, 8, 512),
            scratch(2, 8, 512),
            scratch(2, 12, 8, 512),
            pltpu.VMEM((8, 512), jnp.int32),
            scratch(36, 8, 512),
            scratch(5, 32, 8, 512),
            scratch(5, 32, 8, 512),
            scratch(2, 5, 8, 8, 512),
            scratch(9, 36, 8, 512),
            scratch(2, 5, 8, 512),
            scratch(4, 8, 512),
            scratch(32, 8, 512),
            copies(9),
            copies(4),
            copies(4),
            copies(2, 4),
            copies(4),
            copies(4),
        ],
    )(
        dense,
        dense_1,
        dense_2,
        dense_3,
        sums,
        core,
        layers,
        bc_kind,
        spacing,
        flow_state,
        base,
        far,
        pair,
    )
    ablator_next = call(
        ablate_kernel,
        "ablate",
        struct(64, 1024),
        grant=32,
        in_specs=[SCALARS, ANY] + [VMEM] * 5,
    )(diffuse, final_done, cells, rank, zones, back, abl_temp)
    return (state_next, node_shift, ablator_next)


def solution(mesh):
    in_specs = (
        P(None, "wall", "surf", None),
        P("wall", "surf", None),
        P("surf", None),
        P(("surf", "wall")),
        P(("surf", "wall")),
        P(None, ("surf", "wall")),
        P(),
        P(),
        P(),
    )
    out_specs = (P(None, "wall", "surf", None), P("wall", "surf", None), P(None, ("surf", "wall")))
    return jax.shard_map(shards, mesh=mesh, in_specs=in_specs, out_specs=out_specs, check_vma=False)
```

```python
import functools
import jax
import jax.numpy as jnp
from jax import lax
from jax.experimental import pallas as pl
from jax.experimental.pallas import tpu as pltpu
from jax.sharding import PartitionSpec as P

gas = 0.4
time_step = 0.15
viscosity = 0.05
conduction = 0.07
sponge_rate = 0.5
activation = 2.0
radiation = 0.8
recovery = 0.2
far_values = (1.0, 0.5, 0.0, 0.0, 2.625)
diffusivity = (viscosity, viscosity, viscosity, conduction)

F32 = jnp.float32
BF16 = jnp.bfloat16


def iota(shape, axis):
    return lax.broadcasted_iota(jnp.int32, shape, axis)


def split3(x):
    high = x.astype(BF16)
    rest = x - high.astype(F32)
    middle = rest.astype(BF16)
    low = (rest - middle.astype(F32)).astype(BF16)
    return high, middle, low


def dot_nn(a, b):
    return lax.dot_general(a, b, (((1,), (0,)), ((), ())), preferred_element_type=F32)


def dot_nt(a, b):
    return lax.dot_general(a, b, (((1,), (1,)), ((), ())), preferred_element_type=F32)


def join3(x, rows):
    return x[:rows] + x[rows : 2 * rows] + x[2 * rows :]


def to_rows(x):
    return jnp.concatenate([x[:, 128 * c : 128 * c + 128] for c in range(4)], axis=0)


def to_grid(x):
    return jnp.concatenate([x[8 * c : 8 * c + 8] for c in range(4)], axis=1)


def onehot(mask):
    return jnp.where(mask, 1.0, 0.0).astype(BF16)


def primitives(u0, u1, u2, u3, u4):
    inverse = 1.0 / u0
    vx = u1 * inverse
    vy = u2 * inverse
    vz = u3 * inverse
    pressure = gas * (u4 - 0.5 * (u1 * vx + u2 * vy + u3 * vz))
    return inverse, vx, vy, vz, pressure


def start_all(copies):
    for copy in copies:
        copy.start()


def wait_all(copies):
    for copy in copies:
        copy.wait()


def begin_kernel(
    cell_hbm,
    zone_hbm,
    temps_hbm,
    spacing_hbm,
    flow_hbm,
    outgoing,
    rank_out,
    core_wall,
    cross_layers,
    wall_fields,
    pair_hbm,
    cross_hbm,
    cell,
    zone,
    temps,
    spacing,
    flow,
    sides,
    small_sem,
    in_sem,
    out_sem,
):
    even = lax.axis_index("wall") % 2 == 0
    parity = lax.axis_index("surf") % 2
    small = [
        pltpu.make_async_copy(source, target, small_sem.at[index])
        for index, (source, target) in enumerate(
            (
                (cell_hbm, cell),
                (zone_hbm, zone),
                (temps_hbm.at[pl.ds(0, 8)], temps),
                (spacing_hbm, spacing),
            )
        )
    ]
    loads = [
        pltpu.make_async_copy(chunk_of(flow_hbm, c), chunk_of(flow, c), in_sem.at[c]) for c in range(4)
    ]
    start_all(small)
    start_all(loads)
    row = iota((8, 512), 0) // 2
    stores = []
    for c in range(4):
        loads[c].wait()

        def field(m, carry, c=c):
            for block in (2 * c, 2 * c + 1):
                high = jnp.zeros((8, 512), F32)
                low = jnp.zeros((8, 512), F32)
                for b in range(4):
                    plane = flow[m, block * 4 + b]
                    rolled_high = pltpu.roll(plane, (2 * b + 2) % 8, 0) if b != 3 else plane
                    rolled_low = pltpu.roll(plane, 2 * b, 0) if b else plane
                    high = jnp.where(row == b, rolled_high, high)
                    low = jnp.where(row == b, rolled_low, low)
                sides[0, m, block] = high
                sides[1, m, block] = low
            return carry

        lax.fori_loop(0, 5, field, 0)
        part = pl.ds(2 * c, 2)
        for index, (side, there) in enumerate(((parity, pair_hbm), (1 - parity, cross_hbm))):
            copy = pltpu.make_async_copy(sides.at[side, :, part], there.at[:, part], out_sem.at[index, c])
            copy.start()
            stores.append(copy)
    wait_all(small)
    cells = cell[...]
    tile = cells // 4096
    within = cells - tile * 4096
    hit = iota((32, 1024), 0) == tile
    ones = jnp.where(hit, 1.0, 0.0)
    stacked = jnp.concatenate([ones[:, 128 * k : 128 * k + 128] for k in range(8)], axis=0)
    inner = iota((128, 256), 0)
    outer = iota((128, 256), 1)
    ahead = onehot((inner < outer) | (outer >= 128))
    counts = dot_nn(stacked.astype(BF16), ahead)
    offset = jnp.zeros((32, 128), F32)
    ranks = []
    for k in range(8):
        part = slice(32 * k, 32 * k + 32)
        place = counts[part, :128] + offset
        ranks.append(jnp.sum(stacked[part] * place, axis=0, keepdims=True))
        offset = offset + counts[part, 128:]
    rank = jnp.concatenate(ranks, axis=1).astype(jnp.int32)
    rank_out[...] = rank
    slot = iota((32, 1024), 0) == rank
    first, second = temps[0:1], temps[1:2]
    fields = (within.astype(F32), (zone[...] + 1).astype(F32), first, second)
    pieces = [split3(value) for value in fields]
    rows = []
    for level in range(3):
        for piece in pieces:
            rows.append(jnp.where(slot, piece[level].astype(F32), 0.0).astype(BF16))
    sent = dot_nt(ones.astype(BF16), jnp.concatenate(rows, axis=0))
    outgoing[...] = sent[:, :128] + sent[:, 128:256] + sent[:, 256:]
    layers = [(flow[m, 30 + n], flow[m, n]) for m in range(5) for n in range(2)]
    layers += [(spacing[30 + n], spacing[n]) for n in range(2)]
    for index, (top, bottom) in enumerate(layers):
        core_wall[index] = jnp.where(even, top, bottom)
        cross_layers[index] = jnp.where(even, bottom, top)
    inverse, vx, vy, vz, pressure = primitives(*[flow[m, 0] for m in range(5)])
    film = 2.0 / spacing[0]
    temp = pressure * inverse + recovery * (vx * vx + vy * vy + vz * vz)
    total = spacing[0]
    for k in range(1, 32):
        total = total + spacing[k]
    for index, value in enumerate((film, temp, total)):
        core_wall[12 + index] = value
        wall_fields[index] = value
    wait_all(stores)


def surface_kernel(
    conduct, rate, token, arrived, own, core, twin, cross, dense, sums, where_out
):
    wall = lax.axis_index("wall")
    received = arrived[...]
    pieces = jnp.concatenate(split3(received), axis=0)
    lane = iota((128, 1024), 1) % 32
    line = iota((128, 1024), 0)
    source = iota((32, 1024), 0) == iota((32, 1024), 1) // 32
    flat = []
    for f in range(4):
        spread = join3(dot_nn(pieces, onehot(line == lane + 32 * f)), 32)
        flat.append(jnp.sum(jnp.where(source, spread, 0.0), axis=0, keepdims=True))
    where_out[...] = flat[0]
    cells = flat[0].astype(jnp.int32)
    block = ((cells % 512) // 128) * 8 + cells // 512
    block_hit = iota((32, 1024), 0) == block
    lane_hit = onehot(line == cells % 128)
    rows = [jnp.where(block_hit, flat[1], 0.0).astype(BF16)]
    for value in flat[2:]:
        for piece in split3(value):
            rows.append(jnp.where(block_hit, piece.astype(F32), 0.0).astype(BF16))
    grid = dot_nt(jnp.concatenate(rows, axis=0), lane_hit)
    zones = to_grid(grid[:32])
    surface = to_grid(join3(grid[32:128], 32))
    inner = to_grid(join3(grid[128:], 32))

    def from_bottom(f):
        return jnp.where(
            wall == 0,
            own[f],
            jnp.where(wall == 1, core[12 + f], jnp.where(wall == 2, twin[f], cross[f])),
        )

    sums[0] = (own[2] + core[14]) + (twin[2] + cross[2])
    below = jnp.where(wall % 2 == 1, core[14], 0.0)
    sums[1] = below + jnp.where(wall >= 2, twin[2] + cross[2], 0.0)
    film = from_bottom(0)
    recover = from_bottom(1)
    cond = jnp.zeros((8, 512), F32)
    speed = jnp.zeros((8, 512), F32)
    for z in range(8):
        cond = jnp.where(zones == z + 1.0, conduct[z], cond)
        speed = jnp.where(zones == z + 1.0, rate[z], speed)
    base = film * recover + cond * inner
    for step in range(2):
        cube = surface * surface * surface
        surface = (base + 3.0 * radiation * cube * surface) / (film + cond + 4.0 * radiation * cube)
    recess = speed * jnp.exp(-activation / surface)
    taken = zones > 0.5
    dense[0] = jnp.where(taken, surface, 0.0)
    dense[1] = jnp.where(taken, recess, 0.0)


def return_kernel(where_in, dense, outgoing):
    cells = where_in[...].astype(jnp.int32)
    block = ((cells % 512) // 128) * 8 + cells // 512
    block_hit = iota((32, 1024), 0) == block
    line = iota((128, 1024), 0)
    lane_hit = onehot(line == cells % 128)
    pieces = jnp.concatenate(split3(to_rows(dense[0])), axis=0)
    spread = join3(dot_nn(pieces, lane_hit), 32)
    flat = jnp.sum(jnp.where(block_hit, spread, 0.0), axis=0, keepdims=True)
    source = iota((32, 1024), 0) == iota((32, 1024), 1) // 32
    rows = [jnp.where(source, piece.astype(F32), 0.0).astype(BF16) for piece in split3(flat)]
    slot = onehot(line == iota((128, 1024), 1) % 32)
    outgoing[...] = join3(dot_nt(jnp.concatenate(rows, axis=0), slot), 32)


def ablate_kernel(diffuse, token, cell, rank, zone, back, temps, out):
    pieces = jnp.concatenate(split3(back[...]), axis=0)
    slot = onehot(iota((128, 1024), 0) == rank[...])
    spread = join3(dot_nn(pieces, slot), 32)
    tile_hit = iota((32, 1024), 0) == cell[...] // 4096
    surface = jnp.sum(jnp.where(tile_hit, spread, 0.0), axis=0, keepdims=True)
    zones = zone[...]
    spread_rate = jnp.zeros((1, 1024), F32)
    for z in range(8):
        spread_rate = jnp.where(zones == z, diffuse[z], spread_rate)
    row = iota((64, 1024), 0)
    profile = jnp.where(row == 0, surface, temps[...])
    for step in range(2):
        before = pltpu.roll(profile, 1, 0)
        after = pltpu.roll(profile, 63, 0)
        after = jnp.where(row == 63, before, after)
        changed = profile + spread_rate * (after - 2.0 * profile + before)
        profile = jnp.where(row == 0, profile, changed)
    out[...] = profile


def chunk_of(ref, c):
    return ref.at[:, pl.ds(8 * c, 8)]


TWELFTH = time_step / 12.0


def side_kernel(token, flow_hbm, base_hbm, done, flow, base, in_sem, out_sem):
    done[...] = jnp.zeros_like(done)
    loads = [
        pltpu.make_async_copy(chunk_of(flow_hbm, c), chunk_of(flow, c), in_sem.at[c]) for c in range(4)
    ]
    start_all(loads)
    row = iota((8, 512), 0)
    limits = (row != 7, row != 0, row < 6, row >= 2)

    def one_plane(k, carry):
        u = [flow[m, k] for m in range(5)]
        inverse, vx, vy, vz, pressure = primitives(*u)
        temp = pressure * inverse
        heat = u[4] + pressure
        shear = u[1] * vy
        flux_i = (u[1], u[1] * vx + pressure, shear, u[1] * vz, heat * vx)
        flux_j = (u[2], shear, u[2] * vy + pressure, u[2] * vz, heat * vy)
        smooth = (None, vx, vy, vz, temp)
        for m in range(5):
            result = u[m]
            w = smooth[m]
            if w is not None:
                amount = TWELFTH * diffusivity[m - 1]
                w16 = (16.0 * amount) * w
                w1 = amount * w
                result = result - (60.0 * amount) * w
            for axis, flux in ((0, flux_i[m]), (1, flux_j[m])):
                near = (8.0 * TWELFTH) * flux
                far = TWELFTH * flux
                if w is None:
                    sources = (near, -near, -far, far)
                else:
                    sources = (w16 + near, w16 - near, -w1 - far, far - w1)
                if axis == 0:
                    sources = [jnp.where(limit, value, 0.0) for limit, value in zip(limits, sources)]
                size = (8, 512)[axis]
                for shift, value in zip((1, size - 1, 2, size - 2), sources):
                    result = result + pltpu.roll(value, shift, axis)
            base[m, k] = result
        return carry

    stores = []
    for c in range(4):
        loads[c].wait()
        lax.fori_loop(8 * c, 8 * c + 8, one_plane, 0)
        copy = pltpu.make_async_copy(chunk_of(base, c), chunk_of(base_hbm, c), out_sem.at[c])
        copy.start()
        stores.append(copy)
    wait_all(stores)


def normal_flux(u3, density_x, density_y, vx, vy, vz, pressure, heat):
    return (u3, density_x * vz, density_y * vz, u3 * vz + pressure, heat * vz)


def normal_flux(u3, density_x, density_y, vx, vy, vz, pressure, heat):
    return (u3, density_x * vz, density_y * vz, u3 * vz + pressure, heat * vz)


def final_kernel(
    dense_hbm,
    dense_1_hbm,
    dense_2_hbm,
    dense_3_hbm,
    sums_hbm,
    core_hbm,
    cross_hbm,
    kinds_hbm,
    spacing_hbm,
    flow_hbm,
    base_hbm,
    far_hbm,
    pair_hbm,
    out_hbm,
    shift_hbm,
    done,
    dense,
    sums,
    walls,
    kinds,
    thick,
    flow,
    base,
    sides,
    fields,
    edges,
    run,
    shift,
    small_sem,
    flow_sem,
    base_sem,
    side_sem,
    out_sem,
    shift_sem,
):
    wall = lax.axis_index("wall")
    parity = lax.axis_index("surf") % 2
    odd_wall = wall % 2
    small = [
        pltpu.make_async_copy(source, target, small_sem.at[index])
        for index, (source, target) in enumerate(
            (
                (dense_hbm, dense.at[0]),
                (dense_1_hbm, dense.at[1]),
                (dense_2_hbm, dense.at[2]),
                (dense_3_hbm, dense.at[3]),
                (sums_hbm, sums),
                (core_hbm.at[pl.ds(0, 12)], walls.at[1 - odd_wall]),
                (cross_hbm, walls.at[odd_wall]),
                (kinds_hbm, kinds),
                (spacing_hbm, thick.at[pl.ds(2, 32)]),
            )
        )
    ]
    done[...] = jnp.zeros_like(done)
    start_all(small)

    def flow_load(c):
        return pltpu.make_async_copy(chunk_of(flow_hbm, c), chunk_of(flow, c), flow_sem.at[c])

    def other_loads(c):
        loads = [pltpu.make_async_copy(chunk_of(base_hbm, c), chunk_of(base, c), base_sem.at[c])]
        part = pl.ds(2 * c, 2)
        for index, (source, side) in enumerate(((pair_hbm, 1 - parity), (far_hbm, parity))):
            loads.append(
                pltpu.make_async_copy(source.at[:, part], sides.at[side, :, part], side_sem.at[index, c])
            )
        return loads

    flow_load(0).start()
    for c in range(4):
        if c < 3:
            flow_load(c + 1).start()
        start_all(other_loads(c))
    row = iota((8, 512), 0)
    odd = row % 2 == 1
    is_low = wall == 0
    is_high = wall == 3

    def store_fields(position, flux, smooth):
        for index, value in enumerate(flux + smooth):
            fields[index, position] = value

    def one_field(k, carry):
        u = [flow[m, k] for m in range(5)]
        inverse, vx, vy, vz, pressure = primitives(*u)
        flux = normal_flux(u[3], u[1], u[2], vx, vy, vz, pressure, u[4] + pressure)
        store_fields(k + 2, flux, (vx, vy, vz, pressure * inverse))
        return carry

    def prepare():
        wait_all(small)
        recess = (dense[0, 1] + dense[1, 1]) + (dense[2, 1] + dense[3, 1])
        total = sums[0]
        run[0] = sums[1]
        run[1] = total / (total + recess)
        run[2] = 1.0 / total
        run[3] = recess
        thick[0] = jnp.where(is_low, thick[2], walls[0, 10])
        thick[1] = jnp.where(is_low, thick[3], walls[0, 11])
        thick[34] = jnp.where(is_high, thick[32], walls[1, 10])
        thick[35] = jnp.where(is_high, thick[33], walls[1, 11])
        for layer in range(2):
            u = [jnp.where(is_high, far_values[m], walls[1, 2 * m + layer]) for m in range(5)]
            inverse, vx, vy, vz, pressure = primitives(*u)
            flux = normal_flux(u[3], u[1], u[2], vx, vy, vz, pressure, u[4] + pressure)
            store_fields(34 + layer, flux, (vx, vy, vz, pressure * inverse))
        kind = kinds[...]
        hot = (dense[0, 0] + dense[1, 0]) + (dense[2, 0] + dense[3, 0])
        cooled = 1.0 / hot
        slip = is_low & (kind == 1)
        blow = is_low & (kind == 2)
        sign = jnp.where(is_low, -1.0, 1.0)
        for layer in range(2):
            u = [jnp.where(is_low, flow[m, layer], walls[0, 2 * m + 1 - layer]) for m in range(5)]
            inverse, vx, vy, vz, pressure = primitives(*u)
            density = jnp.where(slip | jnp.logical_not(is_low), u[0], pressure * cooled)
            gx = jnp.where(slip, vx, sign * vx)
            gy = jnp.where(slip, vy, sign * vy)
            gz = jnp.where(blow, 2.0 * recess, 0.0) + sign * vz
            heat = pressure * (1.0 / gas + 1.0) + 0.5 * density * (gx * gx + gy * gy + gz * gz)
            flux = normal_flux(density * gz, density * gx, density * gy, gx, gy, gz, pressure, heat)
            store_fields(1 - layer, flux, (gx, gy, gz, pressure / density))

    def one_block(block, carry):
        for side, near_sign in ((0, 1.0), (1, -1.0)):
            u = [sides[side, m, block] for m in range(5)]
            inverse, vx, vy, vz, pressure = primitives(*u)
            flux = (u[1], u[1] * vx + pressure, u[1] * vy, u[1] * vz, (u[4] + pressure) * vx)
            smooth = (None, vx, vy, vz, pressure * inverse)
            for m in range(5):
                near = (8.0 * TWELFTH * near_sign) * flux[m]
                far = (-TWELFTH * near_sign) * flux[m]
                if smooth[m] is not None:
                    amount = TWELFTH * diffusivity[m - 1]
                    near = near + (16.0 * amount) * smooth[m]
                    far = far - amount * smooth[m]
                if near_sign > 0:
                    moved = jnp.where(odd, 0.0, pltpu.roll(near, 7, 0))
                else:
                    moved = jnp.where(odd, pltpu.roll(near, 1, 0), 0.0)
                edges[side, m] = far + moved
        for b in range(4):
            k = block * 4 + b
            width = thick[k + 2]
            center = run[0] + 0.5 * width
            run[0] = run[0] + width
            normal = center * run[2]
            shift[k] = run[3] * (normal - 1.0)
            stretch = 7.0 * width + 3.0 * (thick[k + 1] + thick[k + 3]) - 0.5 * (thick[k] + thick[k + 4])
            factor = run[1] * (12.0 / stretch)
            damp = (time_step * sponge_rate) * (normal * normal)
            slope_scale = -TWELFTH * factor
            curve_scale = TWELFTH * (factor * factor)
            for m in range(5):
                f = [fields[m, k + o] for o in (0, 1, 3, 4)]
                slope = 8.0 * (f[2] - f[1]) - (f[3] - f[0])
                value = base[m, k] + slope_scale * slope - damp * (flow[m, k] - far_values[m])
                if m:
                    g = [fields[m + 4, k + o] for o in range(5)]
                    curve = 16.0 * (g[1] + g[3]) - (g[0] + g[4]) - 30.0 * g[2]
                    value = value + (curve_scale * diffusivity[m - 1]) * curve
                low_edge = pltpu.roll(edges[0, m], 8 - 2 * b, 0) if b else edges[0, m]
                high_edge = pltpu.roll(edges[1, m], (6 - 2 * b) % 8, 0) if b != 3 else edges[1, m]
                base[m, k] = value + jnp.where(row < 2, low_edge, jnp.where(row >= 6, high_edge, 0.0))
        return carry

    def stores(c):
        rows = pl.ds(8 * c, 8)
        return [
            pltpu.make_async_copy(chunk_of(base, c), chunk_of(out_hbm, c), out_sem.at[c]),
            pltpu.make_async_copy(shift.at[rows], shift_hbm.at[rows], shift_sem.at[c]),
        ]

    def one_chunk(c, carry):
        @pl.when(c < 4)
        def fill():
            flow_load(c).wait()
            lax.fori_loop(8 * c, 8 * c + 8, one_field, 0)

        @pl.when(c == 0)
        def begin():
            prepare()

        @pl.when(c > 0)
        def finish():
            wait_all(other_loads(c - 1))
            lax.fori_loop(2 * c - 2, 2 * c, one_block, 0)
            start_all(stores(c - 1))

        return carry

    lax.fori_loop(0, 5, one_chunk, 0)
    for c in range(4):
        wait_all(stores(c))


def whole(shape):
    return pl.BlockSpec(shape, lambda *_: (0,) * len(shape))


SCALARS = pl.BlockSpec(memory_space=pltpu.SMEM)
ANY = pl.BlockSpec(memory_space=pl.ANY)
HBM = pl.BlockSpec(memory_space=pltpu.HBM)
VMEM = pl.BlockSpec(memory_space=pltpu.VMEM)


def params(grant):
    return pltpu.CompilerParams(vmem_limit_bytes=grant * 1024 * 1024)


def cost():
    return pl.CostEstimate(flops=1000, transcendentals=0, bytes_accessed=1000)


def struct(*shape, dtype=F32):
    return jax.ShapeDtypeStruct(shape, dtype)


def call(kernel, name, out_shape, grant=62, **options):
    return pl.pallas_call(
        kernel,
        out_shape=out_shape,
        name=name,
        compiler_params=params(grant),
        cost_estimate=cost(),
        **options,
    )


def scratch(*shape):
    return pltpu.VMEM(shape, F32)


def copies(*shape):
    return pltpu.SemaphoreType.DMA(shape)


def shards(flow_state, spacing, bc_kind, cell_of, zone_id, abl_temp, conduct, diffuse, rate):
    surf_count = lax.axis_size("surf")
    cells = cell_of.reshape(1, 1024)
    zones = zone_id.reshape(1, 1024)

    def swap(value, axis, partner):
        return lax.ppermute(value, axis, [(i, partner(i)) for i in range(lax.axis_size(axis))])

    outgoing, rank, core_wall, cross_layers, wall_fields, pair_side, cross_side = call(
        begin_kernel,
        "begin",
        (
            struct(32, 128),
            struct(1, 1024, dtype=jnp.int32),
            struct(15, 8, 512),
            struct(12, 8, 512),
            struct(3, 8, 512),
            struct(5, 8, 8, 512),
            struct(5, 8, 8, 512),
        ),
        in_specs=[ANY] * 5,
        out_specs=(VMEM,) * 5 + (ANY,) * 2,
        scratch_shapes=[
            pltpu.VMEM((1, 1024), jnp.int32),
            pltpu.VMEM((1, 1024), jnp.int32),
            scratch(8, 1024),
            scratch(32, 8, 512),
            scratch(5, 32, 8, 512),
            scratch(2, 5, 8, 8, 512),
            copies(4),
            copies(4),
            copies(2, 4),
        ],
    )(cells, zones, abl_temp, spacing, flow_state)
    arrived = lax.all_to_all(outgoing, "surf", split_axis=0, concat_axis=0, tiled=True)
    cross = swap(wall_fields, "wall", lambda i: i ^ 3)
    twin = swap(wall_fields, "wall", lambda i: i ^ 2)
    core = swap(core_wall, "wall", lambda i: i ^ 1)
    far = swap(cross_side, "surf", lambda i: (i - 1 + 2 * (i % 2)) % surf_count)
    pair = swap(pair_side, "surf", lambda i: i ^ 1)
    base, side_done = call(
        side_kernel,
        "side",
        (struct(5, 32, 8, 512), struct(8, 128)),
        in_specs=[ANY, HBM],
        out_specs=(HBM, VMEM),
        scratch_shapes=[scratch(5, 32, 8, 512), scratch(5, 32, 8, 512), copies(4), copies(4)],
    )(rank, flow_state)
    dense, sums, where_cells = call(
        surface_kernel,
        "surface",
        (struct(2, 8, 512), struct(2, 8, 512), struct(1, 1024)),
        grant=32,
        in_specs=[SCALARS] * 2 + [ANY] + [VMEM] * 5,
    )(conduct, rate, side_done, arrived, wall_fields, core, twin, cross)
    cross_layers, where_cells = lax.optimization_barrier((cross_layers, where_cells))
    layers = lax.ppermute(cross_layers, "wall", [(1, 2), (2, 1)])
    dense_1, dense_2, dense_3 = (swap(dense, "wall", lambda i, by=by: i ^ by) for by in (1, 2, 3))
    returned = call(return_kernel, "answer", struct(32, 128), grant=32)(where_cells, dense)
    back = lax.all_to_all(returned, "surf", split_axis=0, concat_axis=0, tiled=True)
    state_next, node_shift, final_done = call(
        final_kernel,
        "final",
        (struct(5, 32, 8, 512), struct(32, 8, 512), struct(8, 128)),
        grant=52,
        in_specs=[ANY] * 8 + [HBM] * 5,
        out_specs=(HBM, HBM, VMEM),
        scratch_shapes=[
            scratch(4, 2, 8, 512),
            scratch(2, 8, 512),
            scratch(2, 12, 8, 512),
            pltpu.VMEM((8, 512), jnp.int32),
            scratch(36, 8, 512),
            scratch(5, 32, 8, 512),
            scratch(5, 32, 8, 512),
            scratch(2, 5, 8, 8, 512),
            scratch(9, 36, 8, 512),
            scratch(2, 5, 8, 512),
            scratch(4, 8, 512),
            scratch(32, 8, 512),
            copies(9),
            copies(4),
            copies(4),
            copies(2, 4),
            copies(4),
            copies(4),
        ],
    )(
        dense,
        dense_1,
        dense_2,
        dense_3,
        sums,
        core,
        layers,
        bc_kind,
        spacing,
        flow_state,
        base,
        far,
        pair,
    )
    ablator_next = call(
        ablate_kernel,
        "ablate",
        struct(64, 1024),
        grant=32,
        in_specs=[SCALARS, ANY] + [VMEM] * 5,
    )(diffuse, final_done, cells, rank, zones, back, abl_temp)
    return (state_next, node_shift, ablator_next)


def solution(mesh):
    in_specs = (
        P(None, "wall", "surf", None),
        P("wall", "surf", None),
        P("surf", None),
        P(("surf", "wall")),
        P(("surf", "wall")),
        P(None, ("surf", "wall")),
        P(),
        P(),
        P(),
    )
    out_specs = (P(None, "wall", "surf", None), P("wall", "surf", None), P(None, ("surf", "wall")))
    return jax.shard_map(shards, mesh=mesh, in_specs=in_specs, out_specs=out_specs, check_vma=False)
```

```python
import functools
import jax
import jax.numpy as jnp
from jax import lax
from jax.experimental import pallas as pl
from jax.experimental.pallas import tpu as pltpu
from jax.sharding import PartitionSpec as P

gas = 0.4
time_step = 0.15
viscosity = 0.05
conduction = 0.07
sponge_rate = 0.5
activation = 2.0
radiation = 0.8
recovery = 0.2
far_values = (1.0, 0.5, 0.0, 0.0, 2.625)
diffusivity = (viscosity, viscosity, viscosity, conduction)

F32 = jnp.float32
BF16 = jnp.bfloat16


def iota(shape, axis):
    return lax.broadcasted_iota(jnp.int32, shape, axis)


def split3(x):
    high = x.astype(BF16)
    rest = x - high.astype(F32)
    middle = rest.astype(BF16)
    low = (rest - middle.astype(F32)).astype(BF16)
    return high, middle, low


def dot_nn(a, b):
    return lax.dot_general(a, b, (((1,), (0,)), ((), ())), preferred_element_type=F32)


def dot_nt(a, b):
    return lax.dot_general(a, b, (((1,), (1,)), ((), ())), preferred_element_type=F32)


def join3(x, rows):
    return x[:rows] + x[rows : 2 * rows] + x[2 * rows :]


def to_rows(x):
    return jnp.concatenate([x[:, 128 * c : 128 * c + 128] for c in range(4)], axis=0)


def to_grid(x):
    return jnp.concatenate([x[8 * c : 8 * c + 8] for c in range(4)], axis=1)


def onehot(mask):
    return jnp.where(mask, 1.0, 0.0).astype(BF16)


def primitives(u0, u1, u2, u3, u4):
    inverse = 1.0 / u0
    vx = u1 * inverse
    vy = u2 * inverse
    vz = u3 * inverse
    pressure = gas * (u4 - 0.5 * (u1 * vx + u2 * vy + u3 * vz))
    return inverse, vx, vy, vz, pressure


def start_all(copies):
    for copy in copies:
        copy.start()


def wait_all(copies):
    for copy in copies:
        copy.wait()


def begin_kernel(
    cell_hbm,
    zone_hbm,
    temps_hbm,
    spacing_hbm,
    flow_hbm,
    outgoing,
    rank_out,
    core_wall,
    cross_layers,
    wall_fields,
    pair_hbm,
    cross_hbm,
    cell,
    zone,
    temps,
    spacing,
    flow,
    sides,
    small_sem,
    in_sem,
    out_sem,
):
    even = lax.axis_index("wall") % 2 == 0
    parity = lax.axis_index("surf") % 2
    small = [
        pltpu.make_async_copy(source, target, small_sem.at[index])
        for index, (source, target) in enumerate(
            (
                (cell_hbm, cell),
                (zone_hbm, zone),
                (temps_hbm.at[pl.ds(0, 8)], temps),
                (spacing_hbm, spacing),
            )
        )
    ]
    loads = [
        pltpu.make_async_copy(chunk_of(flow_hbm, c), chunk_of(flow, c), in_sem.at[c]) for c in range(4)
    ]
    start_all(small)
    start_all(loads)
    row = iota((8, 512), 0) // 2
    stores = []
    for c in range(4):
        loads[c].wait()

        def field(m, carry, c=c):
            for block in (2 * c, 2 * c + 1):
                high = jnp.zeros((8, 512), F32)
                low = jnp.zeros((8, 512), F32)
                for b in range(4):
                    plane = flow[m, block * 4 + b]
                    rolled_high = pltpu.roll(plane, (2 * b + 2) % 8, 0) if b != 3 else plane
                    rolled_low = pltpu.roll(plane, 2 * b, 0) if b else plane
                    high = jnp.where(row == b, rolled_high, high)
                    low = jnp.where(row == b, rolled_low, low)
                sides[0, m, block] = high
                sides[1, m, block] = low
            return carry

        lax.fori_loop(0, 5, field, 0)
        part = pl.ds(2 * c, 2)
        for index, (side, there) in enumerate(((parity, pair_hbm), (1 - parity, cross_hbm))):
            copy = pltpu.make_async_copy(sides.at[side, :, part], there.at[:, part], out_sem.at[index, c])
            copy.start()
            stores.append(copy)
    wait_all(small)
    cells = cell[...]
    tile = cells // 4096
    within = cells - tile * 4096
    hit = iota((32, 1024), 0) == tile
    ones = jnp.where(hit, 1.0, 0.0)
    stacked = jnp.concatenate([ones[:, 128 * k : 128 * k + 128] for k in range(8)], axis=0)
    inner = iota((128, 256), 0)
    outer = iota((128, 256), 1)
    ahead = onehot((inner < outer) | (outer >= 128))
    counts = dot_nn(stacked.astype(BF16), ahead)
    offset = jnp.zeros((32, 128), F32)
    ranks = []
    for k in range(8):
        part = slice(32 * k, 32 * k + 32)
        place = counts[part, :128] + offset
        ranks.append(jnp.sum(stacked[part] * place, axis=0, keepdims=True))
        offset = offset + counts[part, 128:]
    rank = jnp.concatenate(ranks, axis=1).astype(jnp.int32)
    rank_out[...] = rank
    slot = iota((32, 1024), 0) == rank
    first, second = temps[0:1], temps[1:2]
    fields = (within.astype(F32), (zone[...] + 1).astype(F32), first, second)
    pieces = [split3(value) for value in fields]
    rows = []
    for level in range(3):
        for piece in pieces:
            rows.append(jnp.where(slot, piece[level].astype(F32), 0.0).astype(BF16))
    sent = dot_nt(ones.astype(BF16), jnp.concatenate(rows, axis=0))
    outgoing[...] = sent[:, :128] + sent[:, 128:256] + sent[:, 256:]
    layers = [(flow[m, 30 + n], flow[m, n]) for m in range(5) for n in range(2)]
    layers += [(spacing[30 + n], spacing[n]) for n in range(2)]
    for index, (top, bottom) in enumerate(layers):
        core_wall[index] = jnp.where(even, top, bottom)
        cross_layers[index] = jnp.where(even, bottom, top)
    inverse, vx, vy, vz, pressure = primitives(*[flow[m, 0] for m in range(5)])
    film = 2.0 / spacing[0]
    temp = pressure * inverse + recovery * (vx * vx + vy * vy + vz * vz)
    total = spacing[0]
    for k in range(1, 32):
        total = total + spacing[k]
    for index, value in enumerate((film, temp, total)):
        core_wall[12 + index] = value
        wall_fields[index] = value
    wait_all(stores)


def surface_kernel(
    conduct, rate, token, arrived, own, core, twin, cross, dense, sums, where_out
):
    wall = lax.axis_index("wall")
    received = arrived[...]
    pieces = jnp.concatenate(split3(received), axis=0)
    line = iota((128, 1024), 0)
    source = iota((32, 1024), 0) == iota((32, 1024), 1) // 32
    slots = onehot(iota((32, 1024), 0) == iota((32, 1024), 1) % 32)
    flat = []
    for f in range(4):
        spread = join3(dot_nn(pieces[:, 32 * f : 32 * f + 32], slots), 32)
        flat.append(jnp.sum(jnp.where(source, spread, 0.0), axis=0, keepdims=True))
    where_out[...] = flat[0]
    cells = flat[0].astype(jnp.int32)
    block = ((cells % 512) // 128) * 8 + cells // 512
    block_hit = iota((32, 1024), 0) == block
    lane_hit = onehot(line == cells % 128)
    rows = [jnp.where(block_hit, flat[1], 0.0).astype(BF16)]
    for value in flat[2:]:
        for piece in split3(value):
            rows.append(jnp.where(block_hit, piece.astype(F32), 0.0).astype(BF16))
    grid = dot_nt(jnp.concatenate(rows, axis=0), lane_hit)
    zones = to_grid(grid[:32])
    surface = to_grid(join3(grid[32:128], 32))
    inner = to_grid(join3(grid[128:], 32))

    def from_bottom(f):
        return jnp.where(
            wall == 0,
            own[f],
            jnp.where(wall == 1, core[12 + f], jnp.where(wall == 2, twin[f], cross[f])),
        )

    sums[0] = (own[2] + core[14]) + (twin[2] + cross[2])
    below = jnp.where(wall % 2 == 1, core[14], 0.0)
    sums[1] = below + jnp.where(wall >= 2, twin[2] + cross[2], 0.0)
    film = from_bottom(0)
    recover = from_bottom(1)
    cond = jnp.zeros((8, 512), F32)
    speed = jnp.zeros((8, 512), F32)
    for z in range(8):
        cond = jnp.where(zones == z + 1.0, conduct[z], cond)
        speed = jnp.where(zones == z + 1.0, rate[z], speed)
    base = film * recover + cond * inner
    for step in range(2):
        cube = surface * surface * surface
        surface = (base + 3.0 * radiation * cube * surface) / (film + cond + 4.0 * radiation * cube)
    recess = speed * jnp.exp(-activation / surface)
    taken = zones > 0.5
    dense[0] = jnp.where(taken, surface, 0.0)
    dense[1] = jnp.where(taken, recess, 0.0)


def return_kernel(where_in, dense, outgoing):
    cells = where_in[...].astype(jnp.int32)
    block = ((cells % 512) // 128) * 8 + cells // 512
    block_hit = iota((32, 1024), 0) == block
    line = iota((128, 1024), 0)
    lane_hit = onehot(line == cells % 128)
    pieces = jnp.concatenate(split3(to_rows(dense[0])), axis=0)
    spread = join3(dot_nn(pieces, lane_hit), 32)
    flat = jnp.sum(jnp.where(block_hit, spread, 0.0), axis=0, keepdims=True)
    source = iota((32, 1024), 0) == iota((32, 1024), 1) // 32
    rows = [jnp.where(source, piece.astype(F32), 0.0).astype(BF16) for piece in split3(flat)]
    slot = onehot(line == iota((128, 1024), 1) % 32)
    outgoing[...] = join3(dot_nt(jnp.concatenate(rows, axis=0), slot), 32)


def ablate_kernel(diffuse, token, cell, rank, zone, back, temps, out):
    pieces = jnp.concatenate(split3(back[...]), axis=0)[:, :32]
    slot = onehot(iota((32, 1024), 0) == rank[...])
    spread = join3(dot_nn(pieces, slot), 32)
    tile_hit = iota((32, 1024), 0) == cell[...] // 4096
    surface = jnp.sum(jnp.where(tile_hit, spread, 0.0), axis=0, keepdims=True)
    zones = zone[...]
    spread_rate = jnp.zeros((1, 1024), F32)
    for z in range(8):
        spread_rate = jnp.where(zones == z, diffuse[z], spread_rate)
    row = iota((64, 1024), 0)
    profile = jnp.where(row == 0, surface, temps[...])
    for step in range(2):
        before = pltpu.roll(profile, 1, 0)
        after = pltpu.roll(profile, 63, 0)
        after = jnp.where(row == 63, before, after)
        changed = profile + spread_rate * (after - 2.0 * profile + before)
        profile = jnp.where(row == 0, profile, changed)
    out[...] = profile


def chunk_of(ref, c):
    return ref.at[:, pl.ds(8 * c, 8)]


TWELFTH = time_step / 12.0


def side_kernel(token, flow_hbm, base_hbm, done, flow, base, in_sem, out_sem):
    done[...] = jnp.zeros_like(done)
    loads = [
        pltpu.make_async_copy(chunk_of(flow_hbm, c), chunk_of(flow, c), in_sem.at[c]) for c in range(4)
    ]
    start_all(loads)
    row = iota((8, 512), 0)
    limits = (row != 7, row != 0, row < 6, row >= 2)

    def one_plane(k, carry):
        u = [flow[m, k] for m in range(5)]
        inverse, vx, vy, vz, pressure = primitives(*u)
        temp = pressure * inverse
        heat = u[4] + pressure
        shear = u[1] * vy
        flux_i = (u[1], u[1] * vx + pressure, shear, u[1] * vz, heat * vx)
        flux_j = (u[2], shear, u[2] * vy + pressure, u[2] * vz, heat * vy)
        smooth = (None, vx, vy, vz, temp)
        for m in range(5):
            result = u[m]
            w = smooth[m]
            if w is not None:
                amount = TWELFTH * diffusivity[m - 1]
                w16 = (16.0 * amount) * w
                w1 = amount * w
                result = result - (60.0 * amount) * w
            for axis, flux in ((0, flux_i[m]), (1, flux_j[m])):
                near = (8.0 * TWELFTH) * flux
                far = TWELFTH * flux
                if w is None:
                    sources = (near, -near, -far, far)
                else:
                    sources = (w16 + near, w16 - near, -w1 - far, far - w1)
                if axis == 0:
                    sources = [jnp.where(limit, value, 0.0) for limit, value in zip(limits, sources)]
                size = (8, 512)[axis]
                for shift, value in zip((1, size - 1, 2, size - 2), sources):
                    result = result + pltpu.roll(value, shift, axis)
            base[m, k] = result
        return carry

    stores = []
    for c in range(4):
        loads[c].wait()
        lax.fori_loop(8 * c, 8 * c + 8, one_plane, 0)
        copy = pltpu.make_async_copy(chunk_of(base, c), chunk_of(base_hbm, c), out_sem.at[c])
        copy.start()
        stores.append(copy)
    wait_all(stores)


def normal_flux(u3, density_x, density_y, vx, vy, vz, pressure, heat):
    return (u3, density_x * vz, density_y * vz, u3 * vz + pressure, heat * vz)


def normal_flux(u3, density_x, density_y, vx, vy, vz, pressure, heat):
    return (u3, density_x * vz, density_y * vz, u3 * vz + pressure, heat * vz)


def final_kernel(
    dense_hbm,
    dense_1_hbm,
    dense_2_hbm,
    dense_3_hbm,
    sums_hbm,
    core_hbm,
    cross_hbm,
    kinds_hbm,
    spacing_hbm,
    flow_hbm,
    base_hbm,
    far_hbm,
    pair_hbm,
    out_hbm,
    shift_hbm,
    done,
    dense,
    sums,
    walls,
    kinds,
    thick,
    flow,
    base,
    sides,
    fields,
    edges,
    run,
    shift,
    small_sem,
    flow_sem,
    base_sem,
    side_sem,
    out_sem,
    shift_sem,
):
    wall = lax.axis_index("wall")
    parity = lax.axis_index("surf") % 2
    odd_wall = wall % 2
    small = [
        pltpu.make_async_copy(source, target, small_sem.at[index])
        for index, (source, target) in enumerate(
            (
                (dense_hbm, dense.at[0]),
                (dense_1_hbm, dense.at[1]),
                (dense_2_hbm, dense.at[2]),
                (dense_3_hbm, dense.at[3]),
                (sums_hbm, sums),
                (core_hbm.at[pl.ds(0, 12)], walls.at[1 - odd_wall]),
                (cross_hbm, walls.at[odd_wall]),
                (kinds_hbm, kinds),
                (spacing_hbm, thick.at[pl.ds(2, 32)]),
            )
        )
    ]
    done[...] = jnp.zeros_like(done)
    start_all(small)

    def flow_load(c):
        return pltpu.make_async_copy(chunk_of(flow_hbm, c), chunk_of(flow, c), flow_sem.at[c])

    def other_loads(c):
        loads = [pltpu.make_async_copy(chunk_of(base_hbm, c), chunk_of(base, c), base_sem.at[c])]
        part = pl.ds(2 * c, 2)
        for index, (source, side) in enumerate(((pair_hbm, 1 - parity), (far_hbm, parity))):
            loads.append(
                pltpu.make_async_copy(source.at[:, part], sides.at[side, :, part], side_sem.at[index, c])
            )
        return loads

    flow_load(0).start()
    for c in range(4):
        if c < 3:
            flow_load(c + 1).start()
        start_all(other_loads(c))
    row = iota((8, 512), 0)
    odd = row % 2 == 1
    is_low = wall == 0
    is_high = wall == 3

    def store_fields(position, flux, smooth):
        for index, value in enumerate(flux + smooth):
            fields[index, position] = value

    def one_field(k, carry):
        u = [flow[m, k] for m in range(5)]
        inverse, vx, vy, vz, pressure = primitives(*u)
        flux = normal_flux(u[3], u[1], u[2], vx, vy, vz, pressure, u[4] + pressure)
        store_fields(k + 2, flux, (vx, vy, vz, pressure * inverse))
        return carry

    def prepare():
        wait_all(small)
        recess = (dense[0, 1] + dense[1, 1]) + (dense[2, 1] + dense[3, 1])
        total = sums[0]
        run[0] = sums[1]
        run[1] = total / (total + recess)
        run[2] = 1.0 / total
        run[3] = recess
        thick[0] = jnp.where(is_low, thick[2], walls[0, 10])
        thick[1] = jnp.where(is_low, thick[3], walls[0, 11])
        thick[34] = jnp.where(is_high, thick[32], walls[1, 10])
        thick[35] = jnp.where(is_high, thick[33], walls[1, 11])
        for layer in range(2):
            u = [jnp.where(is_high, far_values[m], walls[1, 2 * m + layer]) for m in range(5)]
            inverse, vx, vy, vz, pressure = primitives(*u)
            flux = normal_flux(u[3], u[1], u[2], vx, vy, vz, pressure, u[4] + pressure)
            store_fields(34 + layer, flux, (vx, vy, vz, pressure * inverse))
        kind = kinds[...]
        hot = (dense[0, 0] + dense[1, 0]) + (dense[2, 0] + dense[3, 0])
        cooled = 1.0 / hot
        slip = is_low & (kind == 1)
        blow = is_low & (kind == 2)
        sign = jnp.where(is_low, -1.0, 1.0)
        for layer in range(2):
            u = [jnp.where(is_low, flow[m, layer], walls[0, 2 * m + 1 - layer]) for m in range(5)]
            inverse, vx, vy, vz, pressure = primitives(*u)
            density = jnp.where(slip | jnp.logical_not(is_low), u[0], pressure * cooled)
            gx = jnp.where(slip, vx, sign * vx)
            gy = jnp.where(slip, vy, sign * vy)
            gz = jnp.where(blow, 2.0 * recess, 0.0) + sign * vz
            heat = pressure * (1.0 / gas + 1.0) + 0.5 * density * (gx * gx + gy * gy + gz * gz)
            flux = normal_flux(density * gz, density * gx, density * gy, gx, gy, gz, pressure, heat)
            store_fields(1 - layer, flux, (gx, gy, gz, pressure / density))

    def one_block(block, carry):
        for side, near_sign in ((0, 1.0), (1, -1.0)):
            u = [sides[side, m, block] for m in range(5)]
            inverse, vx, vy, vz, pressure = primitives(*u)
            flux = (u[1], u[1] * vx + pressure, u[1] * vy, u[1] * vz, (u[4] + pressure) * vx)
            smooth = (None, vx, vy, vz, pressure * inverse)
            for m in range(5):
                near = (8.0 * TWELFTH * near_sign) * flux[m]
                far = (-TWELFTH * near_sign) * flux[m]
                if smooth[m] is not None:
                    amount = TWELFTH * diffusivity[m - 1]
                    near = near + (16.0 * amount) * smooth[m]
                    far = far - amount * smooth[m]
                if near_sign > 0:
                    moved = jnp.where(odd, 0.0, pltpu.roll(near, 7, 0))
                else:
                    moved = jnp.where(odd, pltpu.roll(near, 1, 0), 0.0)
                edges[side, m] = far + moved
        for b in range(4):
            k = block * 4 + b
            width = thick[k + 2]
            center = run[0] + 0.5 * width
            run[0] = run[0] + width
            normal = center * run[2]
            shift[k] = run[3] * (normal - 1.0)
            stretch = 7.0 * width + 3.0 * (thick[k + 1] + thick[k + 3]) - 0.5 * (thick[k] + thick[k + 4])
            factor = run[1] * (12.0 / stretch)
            damp = (time_step * sponge_rate) * (normal * normal)
            slope_scale = -TWELFTH * factor
            curve_scale = TWELFTH * (factor * factor)
            for m in range(5):
                f = [fields[m, k + o] for o in (0, 1, 3, 4)]
                slope = 8.0 * (f[2] - f[1]) - (f[3] - f[0])
                value = base[m, k] + slope_scale * slope - damp * (flow[m, k] - far_values[m])
                if m:
                    g = [fields[m + 4, k + o] for o in range(5)]
                    curve = 16.0 * (g[1] + g[3]) - (g[0] + g[4]) - 30.0 * g[2]
                    value = value + (curve_scale * diffusivity[m - 1]) * curve
                low_edge = pltpu.roll(edges[0, m], 8 - 2 * b, 0) if b else edges[0, m]
                high_edge = pltpu.roll(edges[1, m], (6 - 2 * b) % 8, 0) if b != 3 else edges[1, m]
                base[m, k] = value + jnp.where(row < 2, low_edge, jnp.where(row >= 6, high_edge, 0.0))
        return carry

    def stores(c):
        rows = pl.ds(8 * c, 8)
        return [
            pltpu.make_async_copy(chunk_of(base, c), chunk_of(out_hbm, c), out_sem.at[c]),
            pltpu.make_async_copy(shift.at[rows], shift_hbm.at[rows], shift_sem.at[c]),
        ]

    def one_chunk(c, carry):
        @pl.when(c < 4)
        def fill():
            flow_load(c).wait()
            lax.fori_loop(8 * c, 8 * c + 8, one_field, 0)

        @pl.when(c == 0)
        def begin():
            prepare()

        @pl.when(c > 0)
        def finish():
            wait_all(other_loads(c - 1))
            lax.fori_loop(2 * c - 2, 2 * c, one_block, 0)
            start_all(stores(c - 1))

        return carry

    lax.fori_loop(0, 5, one_chunk, 0)
    for c in range(4):
        wait_all(stores(c))


def whole(shape):
    return pl.BlockSpec(shape, lambda *_: (0,) * len(shape))


SCALARS = pl.BlockSpec(memory_space=pltpu.SMEM)
ANY = pl.BlockSpec(memory_space=pl.ANY)
HBM = pl.BlockSpec(memory_space=pltpu.HBM)
VMEM = pl.BlockSpec(memory_space=pltpu.VMEM)


def params(grant):
    return pltpu.CompilerParams(vmem_limit_bytes=grant * 1024 * 1024)


def cost():
    return pl.CostEstimate(flops=1000, transcendentals=0, bytes_accessed=1000)


def struct(*shape, dtype=F32):
    return jax.ShapeDtypeStruct(shape, dtype)


def call(kernel, name, out_shape, grant=62, **options):
    return pl.pallas_call(
        kernel,
        out_shape=out_shape,
        name=name,
        compiler_params=params(grant),
        cost_estimate=cost(),
        **options,
    )


def scratch(*shape):
    return pltpu.VMEM(shape, F32)


def copies(*shape):
    return pltpu.SemaphoreType.DMA(shape)


def shards(flow_state, spacing, bc_kind, cell_of, zone_id, abl_temp, conduct, diffuse, rate):
    surf_count = lax.axis_size("surf")
    cells = cell_of.reshape(1, 1024)
    zones = zone_id.reshape(1, 1024)

    def swap(value, axis, partner):
        return lax.ppermute(value, axis, [(i, partner(i)) for i in range(lax.axis_size(axis))])

    outgoing, rank, core_wall, cross_layers, wall_fields, pair_side, cross_side = call(
        begin_kernel,
        "begin",
        (
            struct(32, 128),
            struct(1, 1024, dtype=jnp.int32),
            struct(15, 8, 512),
            struct(12, 8, 512),
            struct(3, 8, 512),
            struct(5, 8, 8, 512),
            struct(5, 8, 8, 512),
        ),
        in_specs=[ANY] * 5,
        out_specs=(VMEM,) * 5 + (ANY,) * 2,
        scratch_shapes=[
            pltpu.VMEM((1, 1024), jnp.int32),
            pltpu.VMEM((1, 1024), jnp.int32),
            scratch(8, 1024),
            scratch(32, 8, 512),
            scratch(5, 32, 8, 512),
            scratch(2, 5, 8, 8, 512),
            copies(4),
            copies(4),
            copies(2, 4),
        ],
    )(cells, zones, abl_temp, spacing, flow_state)
    arrived = lax.all_to_all(outgoing, "surf", split_axis=0, concat_axis=0, tiled=True)
    cross = swap(wall_fields, "wall", lambda i: i ^ 3)
    twin = swap(wall_fields, "wall", lambda i: i ^ 2)
    core = swap(core_wall, "wall", lambda i: i ^ 1)
    far = swap(cross_side, "surf", lambda i: (i - 1 + 2 * (i % 2)) % surf_count)
    pair = swap(pair_side, "surf", lambda i: i ^ 1)
    base, side_done = call(
        side_kernel,
        "side",
        (struct(5, 32, 8, 512), struct(8, 128)),
        in_specs=[ANY, HBM],
        out_specs=(HBM, VMEM),
        scratch_shapes=[scratch(5, 32, 8, 512), scratch(5, 32, 8, 512), copies(4), copies(4)],
    )(rank, flow_state)
    dense, sums, where_cells = call(
        surface_kernel,
        "surface",
        (struct(2, 8, 512), struct(2, 8, 512), struct(1, 1024)),
        grant=32,
        in_specs=[SCALARS] * 2 + [ANY] + [VMEM] * 5,
    )(conduct, rate, side_done, arrived, wall_fields, core, twin, cross)
    cross_layers, where_cells = lax.optimization_barrier((cross_layers, where_cells))
    layers = lax.ppermute(cross_layers, "wall", [(1, 2), (2, 1)])
    dense_1, dense_2, dense_3 = (swap(dense, "wall", lambda i, by=by: i ^ by) for by in (1, 2, 3))
    returned = call(return_kernel, "answer", struct(32, 128), grant=32)(where_cells, dense)
    back = lax.all_to_all(returned, "surf", split_axis=0, concat_axis=0, tiled=True)
    state_next, node_shift, final_done = call(
        final_kernel,
        "final",
        (struct(5, 32, 8, 512), struct(32, 8, 512), struct(8, 128)),
        grant=52,
        in_specs=[ANY] * 8 + [HBM] * 5,
        out_specs=(HBM, HBM, VMEM),
        scratch_shapes=[
            scratch(4, 2, 8, 512),
            scratch(2, 8, 512),
            scratch(2, 12, 8, 512),
            pltpu.VMEM((8, 512), jnp.int32),
            scratch(36, 8, 512),
            scratch(5, 32, 8, 512),
            scratch(5, 32, 8, 512),
            scratch(2, 5, 8, 8, 512),
            scratch(9, 36, 8, 512),
            scratch(2, 5, 8, 512),
            scratch(4, 8, 512),
            scratch(32, 8, 512),
            copies(9),
            copies(4),
            copies(4),
            copies(2, 4),
            copies(4),
            copies(4),
        ],
    )(
        dense,
        dense_1,
        dense_2,
        dense_3,
        sums,
        core,
        layers,
        bc_kind,
        spacing,
        flow_state,
        base,
        far,
        pair,
    )
    ablator_next = call(
        ablate_kernel,
        "ablate",
        struct(64, 1024),
        grant=32,
        in_specs=[SCALARS, ANY] + [VMEM] * 5,
    )(diffuse, final_done, cells, rank, zones, back, abl_temp)
    return (state_next, node_shift, ablator_next)


def solution(mesh):
    in_specs = (
        P(None, "wall", "surf", None),
        P("wall", "surf", None),
        P("surf", None),
        P(("surf", "wall")),
        P(("surf", "wall")),
        P(None, ("surf", "wall")),
        P(),
        P(),
        P(),
    )
    out_specs = (P(None, "wall", "surf", None), P("wall", "surf", None), P(None, ("surf", "wall")))
    return jax.shard_map(shards, mesh=mesh, in_specs=in_specs, out_specs=out_specs, check_vma=False)
```
